256 devices in a mesh: station: 8 (over x, z_hi), tm: 32 (over y, z_lo, core).
Axes of the slice: x: 4, y: 4, z: 8 (z_hi: 2, z_lo: 4; z = z_hi * 4 + z_lo), core: 2. Of those that a mesh axis runs over, the one named last changes fastest.
Arguments:
- features: bfloat16 [4194304, 256], P(('station', 'tm')), may hold values from -8 to 8
- targets: bfloat16 [4194304], P(('station', 'tm')), may hold values from -6 to 6
- station_ids: int32 [4194304], P(('station', 'tm')), may hold values from 0 to 127
- lead_heads: int32 [4194304], P(('station', 'tm')), may hold values from 0 to 15, as said below
- station_weight: float32 [8, 128], P('station'), may hold values from 0.2 to 5
Outputs:
- leverage: float32 [4194304], P(('station', 'tm'))
- zscores: float32 [16, 256], replicated
- inverse_factor: float32 [16, 256, 256], P(None, 'tm')
The draws below stay inside these ranges and needn't reach their ends.
Inputs may be any that keep to these rules, and one draw needn't show every extreme that they name: lead_heads is constant over each aligned block of 1024 rows.
All inputs are finite; a program needn't handle non-finite values.
Results may differ from the reference program's by a relative error of at most 0.008.
Values sent between devices are 32-bit elements; how exact they have to be, the bound alone decides.
No kernel may reach another device: no remote copies, remote signals or barrier semaphores. Data moves between devices by JAX's collectives and lax.ppermute only.
A program may use at most 128 MiB of HBM per device.

```python
import math
import jax
import jax.numpy as jnp
from jax import lax

F = 256
HEADS = 16
NSTAT = 128
BLK = 1024
ROWS = 4194304
N_STATION = 8


def draw_features(key, part):
    first_key = jax.random.fold_in(key, 11)
    second_key = jax.random.fold_in(key, 12)
    base = jax.random.normal(first_key, (ROWS, F), jnp.float32)
    mixing = jnp.eye(F, dtype=jnp.float32) + 0.6 * jax.random.normal(second_key, (F, F), jnp.float32) / math.sqrt(F)
    mixed = jnp.dot(base, mixing)
    return jnp.clip(mixed, -8.0, 8.0).astype(jnp.bfloat16)


def draw_lead_heads(key, part):
    per_block = jax.random.randint(jax.random.fold_in(key, 21), (ROWS // BLK,), 0, HEADS, dtype=jnp.int32)
    return jnp.repeat(per_block, BLK)


def set_ends(array, rng, smallest, high):
    longest = array.shape.index(max(array.shape))
    spots = []
    for shift in (0, 1):
        where = [jax.random.randint(jax.random.fold_in(rng, axis), (), 0, length) for axis, length in enumerate(array.shape)]
        where[longest] = (where[longest] + shift) % array.shape[longest]
        spots.append(tuple(where))
    return array.at[spots[0]].set(smallest).at[spots[1]].set(high)


def levels(own_key, shape, pieces, least, top_value):
    loudness, own = 1.0, jax.random.fold_in(own_key, 6)
    for axis_at, parts in pieces:
        draws = jnp.exp(jax.random.uniform(jax.random.fold_in(own, axis_at), (parts,), jnp.float32, least / len(pieces), top_value / len(pieces)))
        loudness = loudness * jnp.repeat(draws, shape[axis_at] // parts).reshape([-1 if axis == axis_at else 1 for axis in range(len(shape))])
    return loudness


def normal_values(key, extent, scale, limit, pieces=(), kind=jnp.bfloat16):
    loudness = levels(key, extent, pieces, -0.22, 0.18) if pieces else 1.0
    array = jax.random.normal(key, extent, jnp.float32) * scale * loudness
    return jnp.minimum(jnp.maximum(array, -limit), limit).astype(kind)


def setup_inputs(seed: int = 0) -> dict:
    key_of = jax.random.split(jax.random.key(seed), 6)
    features = draw_features(jax.random.fold_in(key_of[5], 71), 0)
    targets = normal_values(key_of[1], (ROWS,), 1.0, 6.0, ((0, 256),))
    station_ids = set_ends(jax.random.randint(key_of[2], (ROWS,), 0, NSTAT), jax.random.fold_in(key_of[2], 1), 0, NSTAT - 1).astype(jnp.int32)
    lead_heads = draw_lead_heads(jax.random.fold_in(key_of[5], 71), 0)
    station_weight = jnp.clip(jnp.exp(math.log(5.0) - 3.218876 * jax.random.uniform(key_of[4], (N_STATION, NSTAT), jnp.float32) ** levels(key_of[4], (N_STATION, NSTAT), ((0, 8),), -0.2, 0.2)), 0.2, 5.0)
    return {"features": features, "targets": targets, "station_ids": station_ids, "lead_heads": lead_heads, "station_weight": station_weight}


def factor_heads(gram_sum, moment):
    feat_width = gram_sum.shape[-1]
    identity = jnp.eye(feat_width, dtype=jnp.float32)
    lower_factor = jnp.linalg.cholesky(gram_sum + identity)
    inverse = lax.linalg.triangular_solve(lower_factor, jnp.broadcast_to(identity, gram_sum.shape), left_side=True, lower=True)
    inner_term = jnp.einsum('hkj,hj->hk', inverse, moment, precision=lax.Precision.HIGHEST)
    coefficient = jnp.einsum('hkj,hk->hj', inverse, inner_term, precision=lax.Precision.HIGHEST)
    spreads = jnp.sqrt(lax.optimization_barrier(jnp.sum(inverse * inverse, axis=1)))
    return (inverse, coefficient / spreads)

def reference(features, targets, station_ids, lead_heads, station_weight):
    groups = (jnp.arange(ROWS) // (ROWS // N_STATION)).astype(jnp.int32)
    row_weight = station_weight[groups, station_ids]
    weighted = (row_weight[:, None] * features).astype(jnp.bfloat16)
    block_count = ROWS // BLK
    feat_blocks = features.reshape(block_count, BLK, F)
    weight_blocks = weighted.reshape(block_count, BLK, F)
    target_blocks = targets.reshape(block_count, BLK)
    block_heads = lead_heads.reshape(block_count, BLK)[:, 0]

    def accumulate(totals, block_item):
        gram_sum, moment = totals
        feat_block, weight_block, target_block, head_now = block_item
        gram_sum = gram_sum.at[head_now].add(jnp.dot(weight_block.T.astype(jnp.float32), feat_block.astype(jnp.float32), preferred_element_type=jnp.float32))
        moment = moment.at[head_now].add(jnp.dot(target_block.astype(jnp.float32), weight_block.astype(jnp.float32), preferred_element_type=jnp.float32))
        return ((gram_sum, moment), None)
    start = (jnp.zeros((HEADS, F, F), jnp.float32), jnp.zeros((HEADS, F), jnp.float32))
    (gram_sum, moment), unused = lax.scan(accumulate, start, (feat_blocks, weight_blocks, target_blocks, block_heads))
    inverse, zscores = factor_heads(gram_sum, moment)
    inverse_low = inverse.astype(jnp.bfloat16)

    def block_leverage(block_item):
        feat_block, head_now = block_item
        projected = jnp.dot(feat_block.astype(jnp.float32), inverse_low[head_now].T.astype(jnp.float32), preferred_element_type=jnp.float32)
        return lax.optimization_barrier(jnp.sum(projected * projected, axis=1))
    lev_blocks = lax.map(block_leverage, (feat_blocks, block_heads))
    leverage = row_weight * lev_blocks.reshape(ROWS) * (ROWS / (HEADS * F))
    inverse_factor = inverse * math.sqrt(ROWS / HEADS)
    return (leverage, zscores, inverse_factor)
```

```python
import functools
import math

import jax
import jax.numpy as jnp
from jax import lax
from jax.experimental import pallas as pl
from jax.experimental.pallas import tpu as pltpu
from jax.sharding import Mesh, PartitionSpec as P

HEADS = 16
BLK = 1024
HALF = 128
PACKED = HALF + 8
EXACT = lax.Precision.HIGHEST
PLANE = ("x", "y")
COLUMN = ("zh", "zl")
COLUMN_SIZE = 8


def dot_nn(a, b):
    return lax.dot_general(
        a, b, (((1,), (0,)), ((), ())), precision=EXACT, preferred_element_type=jnp.float32
    )


def dot_nt(a, b):
    return lax.dot_general(
        a, b, (((1,), (1,)), ((), ())), precision=EXACT, preferred_element_type=jnp.float32
    )


def square_iotas():
    row_at = lax.broadcasted_iota(jnp.int32, (HALF, HALF), 0)
    col_at = lax.broadcasted_iota(jnp.int32, (HALF, HALF), 1)
    return row_at, col_at


def row_weights(table, ids):
    return jnp.take_along_axis(jnp.broadcast_to(table, ids.shape), ids, axis=1)


def gram_kernel(
    head_ref, core_ref, table_ref, id_ref, target_ref, feat_ref,
    keep_ref, send_ref, total_ref, moment_ref, pair_ref,
):
    step = pl.program_id(0)
    heads = total_ref.shape[0]

    @pl.when(step == 0)
    def _():
        total_ref[...] = jnp.zeros_like(total_ref)
        moment_ref[...] = jnp.zeros_like(moment_ref)

    weight = row_weights(table_ref[...], id_ref[...])
    target = target_ref[...]
    head = head_ref[step]
    flipped = feat_ref[...].T
    pieces = []
    for s in range(BLK // HALF):
        piece = flipped[:, s * HALF : (s + 1) * HALF].astype(jnp.float32) * weight[s : s + 1, :]
        pieces.append(piece.astype(jnp.bfloat16))
    weighted = jnp.concatenate(pieces, axis=1)
    total_ref[head] += jnp.dot(weighted, feat_ref[...], preferred_element_type=jnp.float32)
    target_row = jnp.concatenate([target[s : s + 1, :] for s in range(BLK // HALF)], axis=1)
    target_row = jnp.broadcast_to(target_row, (8, BLK)).astype(jnp.bfloat16)
    moment_ref[head] += lax.dot_general(
        target_row, weighted, (((1,), (1,)), ((), ())), preferred_element_type=jnp.float32
    )

    @pl.when(step == pl.num_programs(0) - 1)
    def _():
        core = core_ref[0]
        row_at, col_at = square_iotas()
        pair_ref[1, HALF:] = jnp.zeros((8, HALF), jnp.float32)
        for h in range(heads):
            second = total_ref[h, HALF:, HALF:]
            diag = jnp.sum(jnp.where(row_at == col_at, second, 0.0), axis=0, keepdims=True)
            moment = moment_ref[h, 0:1]
            pair_ref[0, :HALF] = total_ref[h, HALF:, :HALF]
            pair_ref[0, HALF:] = jnp.concatenate(
                [diag, moment[:, :HALF], moment[:, HALF:], jnp.zeros((5, HALF), jnp.float32)],
                axis=0,
            )
            pair_ref[1, :HALF] = jnp.where(col_at <= row_at, total_ref[h, :HALF, :HALF], second)
            keep_ref[h] = pair_ref[core]
            send_ref[h] = pair_ref[1 - core]


def gram_of(block_heads, core, table, ids, targets, features):
    rows, width = features.shape
    blocks = rows // BLK
    half = jax.ShapeDtypeStruct((HEADS, PACKED, HALF), jnp.float32)
    half_spec = pl.BlockSpec((HEADS, PACKED, HALF), lambda b, h, c: (0, 0, 0))
    return pl.pallas_call(
        gram_kernel,
        out_shape=(half, half),
        grid_spec=pltpu.PrefetchScalarGridSpec(
            num_scalar_prefetch=2,
            grid=(blocks,),
            in_specs=[
                pl.BlockSpec((1, HALF), lambda b, h, c: (0, 0)),
                pl.BlockSpec((BLK // HALF, HALF), lambda b, h, c: (b, 0)),
                pl.BlockSpec((BLK // HALF, HALF), lambda b, h, c: (b, 0)),
                pl.BlockSpec((BLK, width), lambda b, h, c: (b, 0)),
            ],
            out_specs=(half_spec, half_spec),
            scratch_shapes=[
                pltpu.VMEM((HEADS, width, width), jnp.float32),
                pltpu.VMEM((HEADS, 8, width), jnp.float32),
                pltpu.VMEM((2, PACKED, HALF), jnp.float32),
            ],
        ),
        cost_estimate=pl.CostEstimate(
            flops=2 * rows * width * width, bytes_accessed=2 * rows * width, transcendentals=0
        ),
        name="gram",
    )(block_heads, core, table, ids, targets, features)


def plane_sum_kernel(part_ref, out_ref):
    total = part_ref[0]
    for p in range(1, part_ref.shape[0]):
        total = total + part_ref[p]
    rows = HALF // COLUMN_SIZE
    for d in range(COLUMN_SIZE):
        out_ref[d, :rows] = total[d * rows : (d + 1) * rows]
        out_ref[d, rows:] = total[HALF:]


def column_sum_kernel(part_ref, out_ref, extra_ref):
    total = part_ref[0]
    for p in range(1, part_ref.shape[0]):
        total = total + part_ref[p]
    rows = HALF // COLUMN_SIZE
    for d in range(COLUMN_SIZE):
        out_ref[d] = total[:rows]
    extra_ref[...] = total[rows:]


def whole_call(kernel, out_shape, name, *args):
    vmem = pl.BlockSpec(memory_space=pltpu.VMEM)
    outs = jax.tree.map(lambda _: vmem, out_shape)
    return pl.pallas_call(
        kernel, out_shape=out_shape, in_specs=[vmem] * len(args), out_specs=outs, name=name
    )(*args)


def invert_factor(sym):
    row_at, col_at = square_iotas()
    on_diag = row_at == col_at
    diag_only = jnp.where(on_diag, sym, 0.0)
    scale_row = lax.rsqrt(jnp.sum(diag_only, axis=0, keepdims=True))
    scale_col = lax.rsqrt(jnp.sum(diag_only, axis=1, keepdims=True))
    work = sym * scale_row * scale_col
    tiles = [work[8 * t : 8 * t + 8, :] for t in range(HALF // 8)]
    lane = lax.broadcasted_iota(jnp.int32, (1, HALF), 1)
    sub = lax.broadcasted_iota(jnp.int32, (8, 1), 0)
    for k in range(HALF):
        t0, s0 = divmod(k, 8)
        row = tiles[t0][s0 : s0 + 1, :]
        recip = 1.0 / row[:, k : k + 1]
        scaled = jnp.where(lane == k, 1.0 + recip, row * recip)
        for t in range(t0, HALF // 8):
            col = tiles[t][:, k : k + 1]
            if t == t0:
                if s0 == 7:
                    continue
                col = jnp.where(sub > s0, col, 0.0)
            tiles[t] = tiles[t] - col * scaled
    work = jnp.concatenate(tiles, axis=0)
    pivots = jnp.sum(jnp.where(on_diag, work, 0.0), axis=1, keepdims=True)
    unit = jnp.where(on_diag, 1.0, jnp.where(col_at < row_at, work, 0.0))
    return unit * lax.rsqrt(pivots) * scale_row


def factor_kernel(core_ref, main_ref, extra_ref, other_ref, out_ref):
    row_at, col_at = square_iotas()
    eye = (row_at == col_at).astype(jnp.float32)
    first_core = core_ref[0] == 0
    other = other_ref[:HALF]
    cross = jnp.where(first_core, main_ref[...], other)
    merged = jnp.where(first_core, other, main_ref[...])
    extra = jnp.where(first_core, extra_ref[...], other_ref[HALF:])
    merged_t = merged.T
    first = jnp.where(col_at <= row_at, merged, merged_t) + eye
    second = jnp.where(col_at > row_at, merged, merged_t)
    second = jnp.where(col_at == row_at, extra[0:1], second) + eye
    moment1 = extra[1:2]
    moment2 = extra[2:3]
    inv1 = invert_factor(first)
    low = dot_nt(cross, inv1)
    inv2 = invert_factor(second - dot_nt(low, low))
    inv21 = -dot_nn(inv2, dot_nn(low, inv1))
    inner1 = jnp.sum(inv1 * moment1, axis=1, keepdims=True)
    inner2 = jnp.sum(inv21 * moment1 + inv2 * moment2, axis=1, keepdims=True)
    coef1 = jnp.sum(inv1 * inner1 + inv21 * inner2, axis=0, keepdims=True)
    coef2 = jnp.sum(inv2 * inner2, axis=0, keepdims=True)
    spread1 = jnp.sum(inv1 * inv1 + inv21 * inv21, axis=0, keepdims=True)
    spread2 = jnp.sum(inv2 * inv2, axis=0, keepdims=True)
    extra_out = jnp.concatenate(
        [
            jnp.sum(inv2 * eye, axis=0, keepdims=True),
            coef1 / jnp.sqrt(spread1),
            coef2 / jnp.sqrt(spread2),
            jnp.zeros((5, HALF), jnp.float32),
        ],
        axis=0,
    )
    merged_out = jnp.where(col_at <= row_at, inv1, inv2.T)
    main_out = jnp.where(first_core, inv21, merged_out)
    for p in range(out_ref.shape[0]):
        out_ref[p, :HALF] = main_out
        out_ref[p, HALF:] = extra_out


def factor_of(core, main, extra, other):
    vmem = pl.BlockSpec(memory_space=pltpu.VMEM)
    return pl.pallas_call(
        factor_kernel,
        out_shape=jax.ShapeDtypeStruct((HEADS, PACKED, HALF), jnp.float32),
        in_specs=[pl.BlockSpec(memory_space=pltpu.SMEM), vmem, vmem, vmem],
        out_specs=vmem,
        name="factor",
    )(core, main, extra, other)


def lever_kernel(
    lever_scale, factor_scale, head_ref, place_ref, table_ref, id_ref, own_ref, other_ref, feat_ref,
    out_ref, score_ref, piece_ref, low_ref, full_ref,
):
    step = pl.program_id(0)
    heads = low_ref.shape[0]
    piece_rows = piece_ref.shape[1]

    @pl.when(step == 0)
    def _():
        first_core = place_ref[1] == 0
        row_at, col_at = square_iotas()
        own_rows = pl.ds(pl.multiple_of(place_ref[0] * piece_rows, piece_rows), piece_rows)
        for h in range(heads):
            own = own_ref[h, :HALF]
            other = other_ref[h, :HALF]
            merged = jnp.where(first_core, other, own)
            second = jnp.where(col_at > row_at, merged, 0.0).T
            second = jnp.where(col_at == row_at, own_ref[h, HALF : HALF + 1], second)
            full_ref[h, :HALF, :HALF] = jnp.where(col_at <= row_at, merged, 0.0)
            full_ref[h, :HALF, HALF:] = jnp.zeros((HALF, HALF), jnp.float32)
            full_ref[h, HALF:, :HALF] = jnp.where(first_core, own, other)
            full_ref[h, HALF:, HALF:] = second
            low_ref[h] = full_ref[h].astype(jnp.bfloat16)
            score_ref[h : h + 1, :HALF] = own_ref[h, HALF + 1 : HALF + 2]
            score_ref[h : h + 1, HALF:] = own_ref[h, HALF + 2 : HALF + 3]
            piece_ref[h] = full_ref[h, own_rows, :] * factor_scale

    weight = row_weights(table_ref[...], id_ref[...])
    projected = lax.dot_general(
        low_ref[head_ref[step]],
        feat_ref[...],
        (((1,), (1,)), ((), ())),
        preferred_element_type=jnp.float32,
    )
    squares = jnp.sum(projected * projected, axis=0, keepdims=True)
    squares = jnp.concatenate(
        [squares[:, s * HALF : (s + 1) * HALF] for s in range(BLK // HALF)], axis=0
    )
    out_ref[...] = weight * squares * lever_scale


def lever_of(
    block_heads, place, table, ids, own, other, features, lever_scale, factor_scale, piece_rows
):
    rows, width = features.shape
    blocks = rows // BLK
    return pl.pallas_call(
        functools.partial(lever_kernel, lever_scale, factor_scale),
        out_shape=(
            jax.ShapeDtypeStruct((rows // HALF, HALF), jnp.float32),
            jax.ShapeDtypeStruct((HEADS, width), jnp.float32),
            jax.ShapeDtypeStruct((HEADS, piece_rows, width), jnp.float32),
        ),
        grid_spec=pltpu.PrefetchScalarGridSpec(
            num_scalar_prefetch=2,
            grid=(blocks,),
            in_specs=[
                pl.BlockSpec((1, HALF), lambda b, h, o: (0, 0)),
                pl.BlockSpec((BLK // HALF, HALF), lambda b, h, o: (b, 0)),
                pl.BlockSpec((HEADS, PACKED, HALF), lambda b, h, o: (0, 0, 0)),
                pl.BlockSpec((HEADS, PACKED, HALF), lambda b, h, o: (0, 0, 0)),
                pl.BlockSpec((BLK, width), lambda b, h, o: (b, 0)),
            ],
            out_specs=(
                pl.BlockSpec((BLK // HALF, HALF), lambda b, h, o: (b, 0)),
                pl.BlockSpec((HEADS, width), lambda b, h, o: (0, 0)),
                pl.BlockSpec((HEADS, piece_rows, width), lambda b, h, o: (0, 0, 0)),
            ),
            scratch_shapes=[
                pltpu.VMEM((HEADS, width, width), jnp.bfloat16),
                pltpu.VMEM((HEADS, width, width), jnp.float32),
            ],
        ),
        name="lever",
    )(block_heads, place, table, ids, own, other, features)


def swap_cores(value):
    return lax.ppermute(value, "c", [(0, 1), (1, 0)])


def exchange(value, axes):
    return lax.all_to_all(value, axes, 0, 0, tiled=True)


def local(features, targets, station_ids, lead_heads, station_weight):
    row_count, feat_width = features.shape
    block_count = row_count // BLK
    pieces = lax.axis_size(("y", "zl", "c"))
    total_rows = row_count * lax.axis_size(PLANE + COLUMN + ("c",))
    core = lax.axis_index("c").astype(jnp.int32)
    piece_at = lax.axis_index(("y", "zl", "c")).astype(jnp.int32)
    block_heads = lead_heads.reshape(block_count, BLK)[:, 0]
    ids = station_ids.reshape(row_count // HALF, HALF)
    target_rows = targets.astype(jnp.float32).reshape(row_count // HALF, HALF)
    core_at = core.reshape(1)
    place = jnp.stack([piece_at, core])

    keep, send = gram_of(block_heads, core_at, station_weight, ids, target_rows, features)
    chip = keep + swap_cores(send)
    column_rows = HALF // COLUMN_SIZE
    parts = whole_call(
        plane_sum_kernel,
        jax.ShapeDtypeStruct((COLUMN_SIZE, column_rows + 8, HALF), jnp.float32),
        "plane_sum",
        exchange(chip, PLANE),
    )
    summed, extra = whole_call(
        column_sum_kernel,
        (
            jax.ShapeDtypeStruct((COLUMN_SIZE, column_rows, HALF), jnp.float32),
            jax.ShapeDtypeStruct((8, HALF), jnp.float32),
        ),
        "column_sum",
        exchange(parts, COLUMN),
    )
    main = exchange(summed, COLUMN).reshape(HALF, HALF)
    other = swap_cores(jnp.concatenate([main, extra], axis=0))
    own_inverses = exchange(factor_of(core_at, main, extra, other), PLANE)
    other_inverses = swap_cores(own_inverses)
    leverage, zscores, inverse_factor = lever_of(
        block_heads,
        place,
        station_weight,
        ids,
        own_inverses,
        other_inverses,
        features,
        total_rows / (HEADS * feat_width),
        math.sqrt(total_rows / HEADS),
        feat_width // pieces,
    )
    return (leverage.reshape(row_count), zscores, inverse_factor)


def solution(mesh):
    grid = Mesh(mesh.devices.reshape(4, 2, 4, 4, 2), ("x", "zh", "y", "zl", "c"))
    rows = ("x", "zh", "y", "zl", "c")
    return jax.shard_map(
        local,
        mesh=grid,
        in_specs=(P(rows, None), P(rows), P(rows), P(rows), P(("x", "zh"), None)),
        out_specs=(P(rows), P(), P(None, ("y", "zl", "c"), None)),
        check_vma=False,
    )
```

```python
import functools
import math

import jax
import jax.numpy as jnp
from jax import lax
from jax.experimental import pallas as pl
from jax.experimental.pallas import tpu as pltpu
from jax.sharding import Mesh, PartitionSpec as P

HEADS = 16
BLK = 1024
PER_STEP = 4
HALF = 128
PACKED = HALF + 8
EXACT = lax.Precision.HIGHEST
PLANE = ("x", "y")
COLUMN = ("zh", "zl")
SMALL = 8 << 20
WIDE = 56 << 20
LARGE = 51 << 20


def dot_nn(a, b):
    return lax.dot_general(
        a, b, (((1,), (0,)), ((), ())), precision=EXACT, preferred_element_type=jnp.float32
    )


def dot_nt(a, b):
    return lax.dot_general(
        a, b, (((1,), (1,)), ((), ())), precision=EXACT, preferred_element_type=jnp.float32
    )


def square_iotas():
    row_at = lax.broadcasted_iota(jnp.int32, (HALF, HALF), 0)
    col_at = lax.broadcasted_iota(jnp.int32, (HALF, HALF), 1)
    return row_at, col_at


def row_weights(table, ids):
    return jnp.take_along_axis(jnp.broadcast_to(table, ids.shape), ids, axis=1)


def gram_kernel(
    head_ref, core_ref, table_ref, id_ref, target_ref, feat_ref,
    keep_ref, send_ref, total_ref, moment_ref, pair_ref,
):
    step = pl.program_id(0)
    heads = total_ref.shape[0]

    @pl.when(step == 0)
    def _():
        total_ref[...] = jnp.zeros_like(total_ref)
        moment_ref[...] = jnp.zeros_like(moment_ref)

    table = table_ref[...]
    sublanes = BLK // HALF
    for i in range(PER_STEP):
        lines = slice(i * sublanes, (i + 1) * sublanes)
        feats = feat_ref[i * BLK : (i + 1) * BLK]
        weight = row_weights(table, id_ref[lines])
        target = target_ref[lines].astype(jnp.float32)
        head = head_ref[(step * PER_STEP + i) * BLK]
        flipped = feats.T
        pieces = []
        for s in range(sublanes):
            piece = flipped[:, s * HALF : (s + 1) * HALF].astype(jnp.float32)
            pieces.append((piece * weight[s : s + 1, :]).astype(jnp.bfloat16))
        weighted = jnp.concatenate(pieces, axis=1)
        total_ref[head] += jnp.dot(weighted, feats, preferred_element_type=jnp.float32)
        target_row = jnp.concatenate([target[s : s + 1, :] for s in range(sublanes)], axis=1)
        target_row = jnp.broadcast_to(target_row, (8, BLK)).astype(jnp.bfloat16)
        moment_ref[head] += lax.dot_general(
            target_row, weighted, (((1,), (1,)), ((), ())), preferred_element_type=jnp.float32
        )

    @pl.when(step == pl.num_programs(0) - 1)
    def _():
        core = core_ref[0]
        row_at, col_at = square_iotas()
        pair_ref[1, HALF:] = jnp.zeros((8, HALF), jnp.float32)
        for h in range(heads):
            second = total_ref[h, HALF:, HALF:]
            diag = jnp.sum(jnp.where(row_at == col_at, second, 0.0), axis=0, keepdims=True)
            moment = moment_ref[h, 0:1]
            pair_ref[0, :HALF] = total_ref[h, HALF:, :HALF]
            pair_ref[0, HALF:] = jnp.concatenate(
                [diag, moment[:, :HALF], moment[:, HALF:], jnp.zeros((5, HALF), jnp.float32)],
                axis=0,
            )
            pair_ref[1, :HALF] = jnp.where(col_at <= row_at, total_ref[h, :HALF, :HALF], second)
            keep_ref[h] = pair_ref[core]
            send_ref[h] = pair_ref[1 - core]


def gram_of(lead_heads, core, table, ids, targets, features):
    rows, width = features.shape
    blocks = rows // BLK
    half = jax.ShapeDtypeStruct((HEADS, PACKED, HALF), jnp.float32)
    half_spec = pl.BlockSpec((HEADS, PACKED, HALF), lambda b, h, c: (0, 0, 0))
    return pl.pallas_call(
        gram_kernel,
        out_shape=(half, half),
        grid_spec=pltpu.PrefetchScalarGridSpec(
            num_scalar_prefetch=2,
            grid=(blocks // PER_STEP,),
            in_specs=[
                pl.BlockSpec((1, HALF), lambda b, h, c: (0, 0)),
                pl.BlockSpec((PER_STEP * BLK // HALF, HALF), lambda b, h, c: (b, 0)),
                pl.BlockSpec((PER_STEP * BLK // HALF, HALF), lambda b, h, c: (b, 0)),
                pl.BlockSpec((PER_STEP * BLK, width), lambda b, h, c: (b, 0)),
            ],
            out_specs=(half_spec, half_spec),
            scratch_shapes=[
                pltpu.VMEM((HEADS, width, width), jnp.float32),
                pltpu.VMEM((HEADS, 8, width), jnp.float32),
                pltpu.VMEM((2, PACKED, HALF), jnp.float32),
            ],
        ),
        cost_estimate=pl.CostEstimate(
            flops=2 * rows * width * width, bytes_accessed=2 * rows * width, transcendentals=0
        ),
        compiler_params=pltpu.CompilerParams(vmem_limit_bytes=WIDE),
        name="gram",
    )(lead_heads, core, table, ids, targets, features)


def plane_sum_kernel(part_ref, out_ref):
    total = part_ref[0]
    for p in range(1, part_ref.shape[0]):
        total = total + part_ref[p]
    out_ref[...] = total


def column_sum_kernel(*refs):
    place_ref, *part_refs, out_ref, ordered_ref = refs
    count = len(part_refs)
    for k in range(count):
        ordered_ref[lax.rem(place_ref[0] + k, count)] = part_refs[k][...]
    total = ordered_ref[0]
    for k in range(1, count):
        total = total + ordered_ref[k]
    out_ref[...] = total


def column_sum(place, parts):
    vmem = pl.BlockSpec(memory_space=pltpu.VMEM)
    shape = parts[0].shape
    return pl.pallas_call(
        column_sum_kernel,
        out_shape=jax.ShapeDtypeStruct(shape, jnp.float32),
        in_specs=[pl.BlockSpec(memory_space=pltpu.SMEM)] + [vmem] * len(parts),
        out_specs=vmem,
        scratch_shapes=[pltpu.VMEM((len(parts),) + shape, jnp.float32)],
        compiler_params=pltpu.CompilerParams(vmem_limit_bytes=SMALL),
        name="column_sum",
    )(place, *parts)


def whole_call(kernel, out_shape, name, *args):
    vmem = pl.BlockSpec(memory_space=pltpu.VMEM)
    outs = jax.tree.map(lambda _: vmem, out_shape)
    return pl.pallas_call(
        kernel,
        out_shape=out_shape,
        in_specs=[vmem] * len(args),
        out_specs=outs,
        compiler_params=pltpu.CompilerParams(vmem_limit_bytes=SMALL),
        name=name,
    )(*args)


def invert_factor(sym):
    tiles = [sym[8 * t : 8 * t + 8, :] for t in range(HALF // 8)]
    lane = lax.broadcasted_iota(jnp.int32, (8, HALF), 1)
    sub = lax.broadcasted_iota(jnp.int32, (8, HALF), 0)
    rows = []
    for p in range(HALF // 8):
        inside = (lane >= 8 * p) & (lane < 8 * p + 8)
        cols = [jnp.broadcast_to(tiles[p][:, 8 * p + j : 8 * p + j + 1], (8, HALF)) for j in range(8)]
        below = {
            t: [jnp.broadcast_to(tiles[t][:, 8 * p + j : 8 * p + j + 1], (8, HALF)) for j in range(8)]
            for t in range(p + 1, HALF // 8)
        }
        panel = jnp.where(inside, jnp.where(lane == 8 * p + sub, 1.0, 0.0), tiles[p])
        for t in below:
            tiles[t] = jnp.where(inside, 0.0, tiles[t])
        pivots = jnp.ones((8, HALF), jnp.float32)
        for k in range(8):
            pivot = jnp.broadcast_to(cols[k][k : k + 1], (8, HALF))
            recip = 1.0 / pivot
            pivots = jnp.where(sub == k, pivot, pivots)
            across = [jnp.broadcast_to(cols[j][k : k + 1], (8, HALF)) for j in range(k + 1, 8)]
            row = jnp.broadcast_to(panel[k : k + 1], (8, HALF))
            if k < 7:
                scaled = jnp.where(sub > k, cols[k] * recip, 0.0)
                for j in range(k + 1, 8):
                    cols[j] = cols[j] - scaled * across[j - k - 1]
                panel = panel - scaled * row
            for t in below:
                scaled = below[t][k] * recip
                for j in range(k + 1, 8):
                    below[t][j] = below[t][j] - scaled * across[j - k - 1]
                tiles[t] = tiles[t] - scaled * row
        rows.append(jnp.where(lane <= 8 * p + sub, panel, 0.0) * lax.rsqrt(pivots))
    return jnp.concatenate(rows, axis=0)


def factor_kernel(core_ref, own_ref, other_ref, out_ref):
    row_at, col_at = square_iotas()
    eye = (row_at == col_at).astype(jnp.float32)
    first_core = core_ref[0] == 0
    own = own_ref[:HALF]
    other = other_ref[:HALF]
    cross = jnp.where(first_core, own, other)
    merged = jnp.where(first_core, other, own)
    extra = jnp.where(first_core, own_ref[HALF:], other_ref[HALF:])
    merged_t = merged.T
    first = jnp.where(col_at <= row_at, merged, merged_t) + eye
    second = jnp.where(col_at > row_at, merged, merged_t)
    second = jnp.where(col_at == row_at, extra[0:1], second) + eye
    moment1 = extra[1:2]
    moment2 = extra[2:3]
    inv1 = invert_factor(first)
    low = dot_nt(cross, inv1)
    inv2 = invert_factor(second - dot_nt(low, low))
    inv21 = -dot_nn(inv2, dot_nn(low, inv1))
    inner1 = jnp.sum(inv1 * moment1, axis=1, keepdims=True)
    inner2 = jnp.sum(inv21 * moment1 + inv2 * moment2, axis=1, keepdims=True)
    coef1 = jnp.sum(inv1 * inner1 + inv21 * inner2, axis=0, keepdims=True)
    coef2 = jnp.sum(inv2 * inner2, axis=0, keepdims=True)
    spread1 = jnp.sum(inv1 * inv1 + inv21 * inv21, axis=0, keepdims=True)
    spread2 = jnp.sum(inv2 * inv2, axis=0, keepdims=True)
    extra_out = jnp.concatenate(
        [
            jnp.sum(inv2 * eye, axis=0, keepdims=True),
            coef1 / jnp.sqrt(spread1),
            coef2 / jnp.sqrt(spread2),
            jnp.zeros((5, HALF), jnp.float32),
        ],
        axis=0,
    )
    merged_out = jnp.where(col_at <= row_at, inv1, inv2.T)
    main_out = jnp.where(first_core, inv21, merged_out)
    for p in range(out_ref.shape[0]):
        out_ref[p, :HALF] = main_out
        out_ref[p, HALF:] = extra_out


def factor_of(core, own, other):
    vmem = pl.BlockSpec(memory_space=pltpu.VMEM)
    return pl.pallas_call(
        factor_kernel,
        out_shape=jax.ShapeDtypeStruct((HEADS, PACKED, HALF), jnp.float32),
        in_specs=[pl.BlockSpec(memory_space=pltpu.SMEM), vmem, vmem],
        out_specs=vmem,
        compiler_params=pltpu.CompilerParams(vmem_limit_bytes=SMALL),
        name="factor",
    )(core, own, other)


def lever_kernel(
    lever_scale, factor_scale, head_ref, place_ref, table_ref, id_ref, own_ref, other_ref, feat_ref,
    out_ref, score_ref, piece_ref, low_ref, full_ref,
):
    step = pl.program_id(0)
    heads = low_ref.shape[0]
    piece_rows = piece_ref.shape[1]

    @pl.when(step == 0)
    def _():
        first_core = place_ref[1] == 0
        row_at, col_at = square_iotas()
        own_rows = pl.ds(pl.multiple_of(place_ref[0] * piece_rows, piece_rows), piece_rows)
        for h in range(heads):
            own = own_ref[h, :HALF]
            other = other_ref[h, :HALF]
            merged = jnp.where(first_core, other, own)
            second = jnp.where(col_at > row_at, merged, 0.0).T
            second = jnp.where(col_at == row_at, own_ref[h, HALF : HALF + 1], second)
            full_ref[h, :HALF, :HALF] = jnp.where(col_at <= row_at, merged, 0.0)
            full_ref[h, :HALF, HALF:] = jnp.zeros((HALF, HALF), jnp.float32)
            full_ref[h, HALF:, :HALF] = jnp.where(first_core, own, other)
            full_ref[h, HALF:, HALF:] = second
            low_ref[h] = full_ref[h].astype(jnp.bfloat16)
            score_ref[h : h + 1, :HALF] = own_ref[h, HALF + 1 : HALF + 2]
            score_ref[h : h + 1, HALF:] = own_ref[h, HALF + 2 : HALF + 3]
            piece_ref[h] = full_ref[h, own_rows, :] * factor_scale

    table = table_ref[...]
    sublanes = BLK // HALF
    for i in range(PER_STEP):
        lines = slice(i * sublanes, (i + 1) * sublanes)
        weight = row_weights(table, id_ref[lines])
        projected = lax.dot_general(
            low_ref[head_ref[(step * PER_STEP + i) * BLK]],
            feat_ref[i * BLK : (i + 1) * BLK],
            (((1,), (1,)), ((), ())),
            preferred_element_type=jnp.float32,
        )
        squares = jnp.sum(projected * projected, axis=0, keepdims=True)
        squares = jnp.concatenate(
            [squares[:, s * HALF : (s + 1) * HALF] for s in range(sublanes)], axis=0
        )
        out_ref[lines] = weight * squares * lever_scale


def lever_of(
    lead_heads, place, table, ids, own, other, features, lever_scale, factor_scale, piece_rows
):
    rows, width = features.shape
    blocks = rows // BLK
    return pl.pallas_call(
        functools.partial(lever_kernel, lever_scale, factor_scale),
        out_shape=(
            jax.ShapeDtypeStruct((rows // HALF, HALF), jnp.float32),
            jax.ShapeDtypeStruct((HEADS, width), jnp.float32),
            jax.ShapeDtypeStruct((HEADS, piece_rows, width), jnp.float32),
        ),
        grid_spec=pltpu.PrefetchScalarGridSpec(
            num_scalar_prefetch=2,
            grid=(blocks // PER_STEP,),
            in_specs=[
                pl.BlockSpec((1, HALF), lambda b, h, o: (0, 0)),
                pl.BlockSpec((PER_STEP * BLK // HALF, HALF), lambda b, h, o: (b, 0)),
                pl.BlockSpec((HEADS, PACKED, HALF), lambda b, h, o: (0, 0, 0)),
                pl.BlockSpec((HEADS, PACKED, HALF), lambda b, h, o: (0, 0, 0)),
                pl.BlockSpec((PER_STEP * BLK, width), lambda b, h, o: (b, 0)),
            ],
            out_specs=(
                pl.BlockSpec((PER_STEP * BLK // HALF, HALF), lambda b, h, o: (b, 0)),
                pl.BlockSpec((HEADS, width), lambda b, h, o: (0, 0)),
                pl.BlockSpec((HEADS, piece_rows, width), lambda b, h, o: (0, 0, 0)),
            ),
            scratch_shapes=[
                pltpu.VMEM((HEADS, width, width), jnp.bfloat16),
                pltpu.VMEM((HEADS, width, width), jnp.float32),
            ],
        ),
        compiler_params=pltpu.CompilerParams(vmem_limit_bytes=LARGE),
        name="lever",
    )(lead_heads, place, table, ids, own, other, features)


def swap_cores(value):
    return lax.ppermute(value, "c", [(0, 1), (1, 0)])


def around_column(value):
    count = lax.axis_size(COLUMN)
    up = [(i, (i + 1) % count) for i in range(count)]
    down = [(i, (i - 1) % count) for i in range(count)]
    parts = [value] + [None] * (count - 1)
    for k in range(1, count // 2 + 1):
        parts[count - k] = lax.ppermute(parts[(count - k + 1) % count], COLUMN, up)
        if k < count - k:
            parts[k] = lax.ppermute(parts[k - 1], COLUMN, down)
    return parts


def exchange(value, axes):
    return lax.all_to_all(value, axes, 0, 0, tiled=True)


def local(features, targets, station_ids, lead_heads, station_weight):
    row_count, feat_width = features.shape
    pieces = lax.axis_size(("y", "zl", "c"))
    total_rows = row_count * lax.axis_size(PLANE + COLUMN + ("c",))
    core = lax.axis_index("c").astype(jnp.int32)
    piece_at = lax.axis_index(("y", "zl", "c")).astype(jnp.int32)
    ids = station_ids.reshape(row_count // HALF, HALF)
    target_rows = targets.reshape(row_count // HALF, HALF)
    core_at = core.reshape(1)
    place = jnp.stack([piece_at, core])

    keep, send = gram_of(lead_heads, core_at, station_weight, ids, target_rows, features)
    chip = keep + swap_cores(send)
    partial = whole_call(
        plane_sum_kernel,
        jax.ShapeDtypeStruct((PACKED, HALF), jnp.float32),
        "plane_sum",
        exchange(chip, PLANE),
    )
    own = column_sum(lax.axis_index(COLUMN).astype(jnp.int32).reshape(1), around_column(partial))
    own_inverses = exchange(factor_of(core_at, own, swap_cores(own)), PLANE)
    other_inverses = swap_cores(own_inverses)
    leverage, zscores, inverse_factor = lever_of(
        lead_heads,
        place,
        station_weight,
        ids,
        own_inverses,
        other_inverses,
        features,
        total_rows / (HEADS * feat_width),
        math.sqrt(total_rows / HEADS),
        feat_width // pieces,
    )
    return (leverage.reshape(row_count), zscores, inverse_factor)


def solution(mesh):
    grid = Mesh(mesh.devices.reshape(4, 2, 4, 4, 2), ("x", "zh", "y", "zl", "c"))
    rows = ("x", "zh", "y", "zl", "c")
    return jax.shard_map(
        local,
        mesh=grid,
        in_specs=(P(rows, None), P(rows), P(rows), P(rows), P(("x", "zh"), None)),
        out_specs=(P(rows), P(), P(None, ("y", "zl", "c"), None)),
        check_vma=False,
    )
```

```python
import functools
import math

import jax
import jax.numpy as jnp
from jax import lax
from jax.experimental import pallas as pl
from jax.experimental.pallas import tpu as pltpu
from jax.sharding import Mesh, PartitionSpec as P

HEADS = 16
BLK = 1024
PER_STEP = 4
HALF = 128
PACKED = HALF + 8
EXACT = lax.Precision.HIGHEST
PART = HALF // 2
PIECE = PART + 8
PLANE = ("x", "y")
COLUMN = ("zh", "zm", "z0")
SMALL = 8 << 20
WIDE = 56 << 20
LARGE = 51 << 20


def dot_nn(a, b):
    return lax.dot_general(
        a, b, (((1,), (0,)), ((), ())), precision=EXACT, preferred_element_type=jnp.float32
    )


def dot_nt(a, b):
    return lax.dot_general(
        a, b, (((1,), (1,)), ((), ())), precision=EXACT, preferred_element_type=jnp.float32
    )


def square_iotas():
    row_at = lax.broadcasted_iota(jnp.int32, (HALF, HALF), 0)
    col_at = lax.broadcasted_iota(jnp.int32, (HALF, HALF), 1)
    return row_at, col_at


def row_weights(table, ids):
    return jnp.take_along_axis(jnp.broadcast_to(table, ids.shape), ids, axis=1)


def gram_kernel(
    head_ref, core_ref, table_ref, id_ref, target_ref, feat_ref,
    keep_ref, send_ref, total_ref, moment_ref, pair_ref,
):
    step = pl.program_id(0)
    heads = total_ref.shape[0]

    @pl.when(step == 0)
    def _():
        total_ref[...] = jnp.zeros_like(total_ref)
        moment_ref[...] = jnp.zeros_like(moment_ref)

    table = table_ref[...]
    sublanes = BLK // HALF
    for i in range(PER_STEP):
        lines = slice(i * sublanes, (i + 1) * sublanes)
        feats = feat_ref[i * BLK : (i + 1) * BLK]
        weight = row_weights(table, id_ref[lines])
        target = target_ref[lines].astype(jnp.float32)
        head = head_ref[(step * PER_STEP + i) * BLK]
        flipped = feats.T
        pieces = []
        for s in range(sublanes):
            piece = flipped[:, s * HALF : (s + 1) * HALF].astype(jnp.float32)
            pieces.append((piece * weight[s : s + 1, :]).astype(jnp.bfloat16))
        weighted = jnp.concatenate(pieces, axis=1)
        total_ref[head] += jnp.dot(weighted, feats, preferred_element_type=jnp.float32)
        target_row = jnp.concatenate([target[s : s + 1, :] for s in range(sublanes)], axis=1)
        target_row = jnp.broadcast_to(target_row, (8, BLK)).astype(jnp.bfloat16)
        moment_ref[head] += lax.dot_general(
            target_row, weighted, (((1,), (1,)), ((), ())), preferred_element_type=jnp.float32
        )

    @pl.when(step == pl.num_programs(0) - 1)
    def _():
        core = core_ref[0]
        row_at, col_at = square_iotas()
        pair_ref[1, :, PART:] = jnp.zeros((2, 8, HALF), jnp.float32)
        for h in range(heads):
            second = total_ref[h, HALF:, HALF:]
            diag = jnp.sum(jnp.where(row_at == col_at, second, 0.0), axis=0, keepdims=True)
            moment = moment_ref[h, 0:1]
            extra = jnp.concatenate(
                [diag, moment[:, :HALF], moment[:, HALF:], jnp.zeros((5, HALF), jnp.float32)],
                axis=0,
            )
            merged = jnp.where(col_at <= row_at, total_ref[h, :HALF, :HALF], second)
            for q in range(2):
                pair_ref[0, q, :PART] = total_ref[h, HALF + q * PART : HALF + (q + 1) * PART, :HALF]
                pair_ref[0, q, PART:] = extra
                pair_ref[1, q, :PART] = merged[q * PART : (q + 1) * PART]
            keep_ref[2 * h : 2 * h + 2] = pair_ref[core]
            send_ref[2 * h : 2 * h + 2] = pair_ref[1 - core]


def gram_of(lead_heads, core, table, ids, targets, features):
    rows, width = features.shape
    blocks = rows // BLK
    half = jax.ShapeDtypeStruct((2 * HEADS, PIECE, HALF), jnp.float32)
    half_spec = pl.BlockSpec((2 * HEADS, PIECE, HALF), lambda b, h, c: (0, 0, 0))
    return pl.pallas_call(
        gram_kernel,
        out_shape=(half, half),
        grid_spec=pltpu.PrefetchScalarGridSpec(
            num_scalar_prefetch=2,
            grid=(blocks // PER_STEP,),
            in_specs=[
                pl.BlockSpec((1, HALF), lambda b, h, c: (0, 0)),
                pl.BlockSpec((PER_STEP * BLK // HALF, HALF), lambda b, h, c: (b, 0)),
                pl.BlockSpec((PER_STEP * BLK // HALF, HALF), lambda b, h, c: (b, 0)),
                pl.BlockSpec((PER_STEP * BLK, width), lambda b, h, c: (b, 0)),
            ],
            out_specs=(half_spec, half_spec),
            scratch_shapes=[
                pltpu.VMEM((HEADS, width, width), jnp.float32),
                pltpu.VMEM((HEADS, 8, width), jnp.float32),
                pltpu.VMEM((2, 2, PIECE, HALF), jnp.float32),
            ],
        ),
        cost_estimate=pl.CostEstimate(
            flops=2 * rows * width * width, bytes_accessed=2 * rows * width, transcendentals=0
        ),
        compiler_params=pltpu.CompilerParams(vmem_limit_bytes=WIDE),
        name="gram",
    )(lead_heads, core, table, ids, targets, features)


def plane_sum_kernel(part_ref, out_ref):
    total = part_ref[0]
    for p in range(1, part_ref.shape[0]):
        total = total + part_ref[p]
    for d in range(out_ref.shape[0]):
        out_ref[d] = total


def column_sum_kernel(part_ref, out_ref):
    total = part_ref[0:2]
    for p in range(2, part_ref.shape[0], 2):
        total = total + part_ref[p : p + 2]
    out_ref[:PART] = total[0, :PART]
    out_ref[PART:HALF] = total[1, :PART]
    out_ref[HALF:] = total[0, PART:]


def whole_call(kernel, out_shape, name, *args):
    vmem = pl.BlockSpec(memory_space=pltpu.VMEM)
    outs = jax.tree.map(lambda _: vmem, out_shape)
    return pl.pallas_call(
        kernel,
        out_shape=out_shape,
        in_specs=[vmem] * len(args),
        out_specs=outs,
        compiler_params=pltpu.CompilerParams(vmem_limit_bytes=SMALL),
        name=name,
    )(*args)


def invert_factor(sym):
    tiles = [sym[8 * t : 8 * t + 8, :] for t in range(HALF // 8)]
    lane = lax.broadcasted_iota(jnp.int32, (8, HALF), 1)
    sub = lax.broadcasted_iota(jnp.int32, (8, HALF), 0)
    rows = []
    for p in range(HALF // 8):
        inside = (lane >= 8 * p) & (lane < 8 * p + 8)
        cols = [jnp.broadcast_to(tiles[p][:, 8 * p + j : 8 * p + j + 1], (8, HALF)) for j in range(8)]
        below = {
            t: [jnp.broadcast_to(tiles[t][:, 8 * p + j : 8 * p + j + 1], (8, HALF)) for j in range(8)]
            for t in range(p + 1, HALF // 8)
        }
        panel = jnp.where(inside, jnp.where(lane == 8 * p + sub, 1.0, 0.0), tiles[p])
        for t in below:
            tiles[t] = jnp.where(inside, 0.0, tiles[t])
        pivots = jnp.ones((8, HALF), jnp.float32)
        for k in range(8):
            pivot = jnp.broadcast_to(cols[k][k : k + 1], (8, HALF))
            recip = 1.0 / pivot
            pivots = jnp.where(sub == k, pivot, pivots)
            across = [jnp.broadcast_to(cols[j][k : k + 1], (8, HALF)) for j in range(k + 1, 8)]
            row = jnp.broadcast_to(panel[k : k + 1], (8, HALF))
            if k < 7:
                scaled = jnp.where(sub > k, cols[k] * recip, 0.0)
                for j in range(k + 1, 8):
                    cols[j] = cols[j] - scaled * across[j - k - 1]
                panel = panel - scaled * row
            for t in below:
                scaled = below[t][k] * recip
                for j in range(k + 1, 8):
                    below[t][j] = below[t][j] - scaled * across[j - k - 1]
                tiles[t] = tiles[t] - scaled * row
        rows.append(jnp.where(lane <= 8 * p + sub, panel, 0.0) * lax.rsqrt(pivots))
    return jnp.concatenate(rows, axis=0)


def factor_kernel(core_ref, own_ref, other_ref, out_ref):
    row_at, col_at = square_iotas()
    eye = (row_at == col_at).astype(jnp.float32)
    first_core = core_ref[0] == 0
    own = own_ref[:HALF]
    other = other_ref[:HALF]
    cross = jnp.where(first_core, own, other)
    merged = jnp.where(first_core, other, own)
    extra = jnp.where(first_core, own_ref[HALF:], other_ref[HALF:])
    merged_t = merged.T
    first = jnp.where(col_at <= row_at, merged, merged_t) + eye
    second = jnp.where(col_at > row_at, merged, merged_t)
    second = jnp.where(col_at == row_at, extra[0:1], second) + eye
    moment1 = extra[1:2]
    moment2 = extra[2:3]
    inv1 = invert_factor(first)
    low = dot_nt(cross, inv1)
    inv2 = invert_factor(second - dot_nt(low, low))
    inv21 = -dot_nn(inv2, dot_nn(low, inv1))
    inner1 = jnp.sum(inv1 * moment1, axis=1, keepdims=True)
    inner2 = jnp.sum(inv21 * moment1 + inv2 * moment2, axis=1, keepdims=True)
    coef1 = jnp.sum(inv1 * inner1 + inv21 * inner2, axis=0, keepdims=True)
    coef2 = jnp.sum(inv2 * inner2, axis=0, keepdims=True)
    spread1 = jnp.sum(inv1 * inv1 + inv21 * inv21, axis=0, keepdims=True)
    spread2 = jnp.sum(inv2 * inv2, axis=0, keepdims=True)
    extra_out = jnp.concatenate(
        [
            jnp.sum(inv2 * eye, axis=0, keepdims=True),
            coef1 / jnp.sqrt(spread1),
            coef2 / jnp.sqrt(spread2),
            jnp.zeros((5, HALF), jnp.float32),
        ],
        axis=0,
    )
    merged_out = jnp.where(col_at <= row_at, inv1, inv2.T)
    main_out = jnp.where(first_core, inv21, merged_out)
    for p in range(out_ref.shape[0]):
        out_ref[p, :HALF] = main_out
        out_ref[p, HALF:] = extra_out


def factor_of(core, own, other):
    vmem = pl.BlockSpec(memory_space=pltpu.VMEM)
    return pl.pallas_call(
        factor_kernel,
        out_shape=jax.ShapeDtypeStruct((HEADS, PACKED, HALF), jnp.float32),
        in_specs=[pl.BlockSpec(memory_space=pltpu.SMEM), vmem, vmem],
        out_specs=vmem,
        compiler_params=pltpu.CompilerParams(vmem_limit_bytes=SMALL),
        name="factor",
    )(core, own, other)


def lever_kernel(
    lever_scale, factor_scale, head_ref, place_ref, table_ref, id_ref, own_ref, other_ref, feat_ref,
    out_ref, score_ref, piece_ref, low_ref, full_ref,
):
    step = pl.program_id(0)
    heads = low_ref.shape[0]
    piece_rows = piece_ref.shape[1]

    @pl.when(step == 0)
    def _():
        first_core = place_ref[1] == 0
        row_at, col_at = square_iotas()
        own_rows = pl.ds(pl.multiple_of(place_ref[0] * piece_rows, piece_rows), piece_rows)
        for h in range(heads):
            own = own_ref[h, :HALF]
            other = other_ref[h, :HALF]
            merged = jnp.where(first_core, other, own)
            second = jnp.where(col_at > row_at, merged, 0.0).T
            second = jnp.where(col_at == row_at, own_ref[h, HALF : HALF + 1], second)
            full_ref[h, :HALF, :HALF] = jnp.where(col_at <= row_at, merged, 0.0)
            full_ref[h, :HALF, HALF:] = jnp.zeros((HALF, HALF), jnp.float32)
            full_ref[h, HALF:, :HALF] = jnp.where(first_core, own, other)
            full_ref[h, HALF:, HALF:] = second
            low_ref[h] = full_ref[h].astype(jnp.bfloat16)
            score_ref[h : h + 1, :HALF] = own_ref[h, HALF + 1 : HALF + 2]
            score_ref[h : h + 1, HALF:] = own_ref[h, HALF + 2 : HALF + 3]
            piece_ref[h] = full_ref[h, own_rows, :] * factor_scale

    table = table_ref[...]
    sublanes = BLK // HALF
    for i in range(PER_STEP):
        lines = slice(i * sublanes, (i + 1) * sublanes)
        weight = row_weights(table, id_ref[lines])
        projected = lax.dot_general(
            low_ref[head_ref[(step * PER_STEP + i) * BLK]],
            feat_ref[i * BLK : (i + 1) * BLK],
            (((1,), (1,)), ((), ())),
            preferred_element_type=jnp.float32,
        )
        squares = jnp.sum(projected * projected, axis=0, keepdims=True)
        squares = jnp.concatenate(
            [squares[:, s * HALF : (s + 1) * HALF] for s in range(sublanes)], axis=0
        )
        out_ref[lines] = weight * squares * lever_scale


def lever_of(
    lead_heads, place, table, ids, own, other, features, lever_scale, factor_scale, piece_rows
):
    rows, width = features.shape
    blocks = rows // BLK
    return pl.pallas_call(
        functools.partial(lever_kernel, lever_scale, factor_scale),
        out_shape=(
            jax.ShapeDtypeStruct((rows // HALF, HALF), jnp.float32),
            jax.ShapeDtypeStruct((HEADS, width), jnp.float32),
            jax.ShapeDtypeStruct((HEADS, piece_rows, width), jnp.float32),
        ),
        grid_spec=pltpu.PrefetchScalarGridSpec(
            num_scalar_prefetch=2,
            grid=(blocks // PER_STEP,),
            in_specs=[
                pl.BlockSpec((1, HALF), lambda b, h, o: (0, 0)),
                pl.BlockSpec((PER_STEP * BLK // HALF, HALF), lambda b, h, o: (b, 0)),
                pl.BlockSpec((HEADS, PACKED, HALF), lambda b, h, o: (0, 0, 0)),
                pl.BlockSpec((HEADS, PACKED, HALF), lambda b, h, o: (0, 0, 0)),
                pl.BlockSpec((PER_STEP * BLK, width), lambda b, h, o: (b, 0)),
            ],
            out_specs=(
                pl.BlockSpec((PER_STEP * BLK // HALF, HALF), lambda b, h, o: (b, 0)),
                pl.BlockSpec((HEADS, width), lambda b, h, o: (0, 0)),
                pl.BlockSpec((HEADS, piece_rows, width), lambda b, h, o: (0, 0, 0)),
            ),
            scratch_shapes=[
                pltpu.VMEM((HEADS, width, width), jnp.bfloat16),
                pltpu.VMEM((HEADS, width, width), jnp.float32),
            ],
        ),
        compiler_params=pltpu.CompilerParams(vmem_limit_bytes=LARGE),
        name="lever",
    )(lead_heads, place, table, ids, own, other, features)


def swap_cores(value):
    return lax.ppermute(value, "c", [(0, 1), (1, 0)])


def exchange(value, axes):
    return lax.all_to_all(value, axes, 0, 0, tiled=True)


def local(features, targets, station_ids, lead_heads, station_weight):
    row_count, feat_width = features.shape
    pieces = lax.axis_size(("y", "zm", "z0", "c"))
    total_rows = row_count * lax.axis_size(PLANE + COLUMN + ("c",))
    core = lax.axis_index("c").astype(jnp.int32)
    piece_at = lax.axis_index(("y", "zm", "z0", "c")).astype(jnp.int32)
    ids = station_ids.reshape(row_count // HALF, HALF)
    target_rows = targets.reshape(row_count // HALF, HALF)
    core_at = core.reshape(1)
    place = jnp.stack([piece_at, core])

    keep, send = gram_of(lead_heads, core_at, station_weight, ids, target_rows, features)
    chip = keep + swap_cores(send)
    spread = whole_call(
        plane_sum_kernel,
        jax.ShapeDtypeStruct((lax.axis_size(COLUMN), PIECE, HALF), jnp.float32),
        "plane_sum",
        exchange(chip, PLANE + ("z0",)),
    )
    own = whole_call(
        column_sum_kernel,
        jax.ShapeDtypeStruct((PACKED, HALF), jnp.float32),
        "column_sum",
        exchange(spread, COLUMN),
    )
    own_inverses = exchange(factor_of(core_at, own, swap_cores(own)), PLANE)
    other_inverses = swap_cores(own_inverses)
    leverage, zscores, inverse_factor = lever_of(
        lead_heads,
        place,
        station_weight,
        ids,
        own_inverses,
        other_inverses,
        features,
        total_rows / (HEADS * feat_width),
        math.sqrt(total_rows / HEADS),
        feat_width // pieces,
    )
    return (leverage.reshape(row_count), zscores, inverse_factor)


def solution(mesh):
    grid = Mesh(mesh.devices.reshape(4, 2, 4, 2, 2, 2), ("x", "zh", "y", "zm", "z0", "c"))
    rows = ("x", "zh", "y", "zm", "z0", "c")
    return jax.shard_map(
        local,
        mesh=grid,
        in_specs=(P(rows, None), P(rows), P(rows), P(rows), P(("x", "zh"), None)),
        out_specs=(P(rows), P(), P(None, ("y", "zm", "z0", "c"), None)),
        check_vma=False,
    )
```

```python
import functools
import math

import jax
import jax.numpy as jnp
from jax import lax
from jax.experimental import pallas as pl
from jax.experimental.pallas import tpu as pltpu
from jax.sharding import Mesh, PartitionSpec as P

HEADS = 16
BLK = 1024
PER_STEP = 4
HALF = 128
PACKED = HALF + 8
EXACT = lax.Precision.HIGHEST
PART = HALF // 2
PIECE = PART + 8
PLANE = ("x", "y")
COLUMN = ("zh", "zm", "z0")
SMALL = 8 << 20
WIDE = 56 << 20
LARGE = 51 << 20


def dot_nn(a, b):
    return lax.dot_general(
        a, b, (((1,), (0,)), ((), ())), precision=EXACT, preferred_element_type=jnp.float32
    )


def dot_nt(a, b):
    return lax.dot_general(
        a, b, (((1,), (1,)), ((), ())), precision=EXACT, preferred_element_type=jnp.float32
    )


def square_iotas():
    row_at = lax.broadcasted_iota(jnp.int32, (HALF, HALF), 0)
    col_at = lax.broadcasted_iota(jnp.int32, (HALF, HALF), 1)
    return row_at, col_at


def row_weights(table, ids):
    return jnp.take_along_axis(jnp.broadcast_to(table, ids.shape), ids, axis=1)


def chunk_copy(chunk, rows, source_ref, target_ref, sems):
    lines = pl.ds(pl.multiple_of(chunk * rows, rows), rows)
    return pltpu.make_async_copy(source_ref.at[lines], target_ref.at[lines], sems.at[chunk])


def gram_kernel(
    core_ref, lead_ref, table_ref, id_ref, target_ref, feats_ref,
    keep_ref, send_ref, picked_ref,
    total_ref, moment_ref, pair_ref, feat_ref, head_ref, feat_sems, head_sems,
):
    heads = total_ref.shape[0]
    chunk_rows = PER_STEP * BLK
    chunks = feat_ref.shape[0] // chunk_rows
    for c in range(chunks):
        chunk_copy(c, chunk_rows, lead_ref, head_ref, head_sems).start()
        chunk_copy(c, chunk_rows, feats_ref, feat_ref, feat_sems).start()
    total_ref[...] = jnp.zeros_like(total_ref)
    moment_ref[...] = jnp.zeros_like(moment_ref)
    table = table_ref[...]
    sublanes = BLK // HALF

    def add_chunk(chunk, carry):
        chunk_copy(chunk, chunk_rows, lead_ref, head_ref, head_sems).wait()
        chunk_copy(chunk, chunk_rows, feats_ref, feat_ref, feat_sems).wait()
        for i in range(PER_STEP):
            block = chunk * PER_STEP + i
            lines = pl.ds(pl.multiple_of(block * sublanes, sublanes), sublanes)
            feats = feat_ref[pl.ds(pl.multiple_of(block * BLK, BLK), BLK)]
            weight = row_weights(table, id_ref[lines])
            target = target_ref[lines].astype(jnp.float32)
            head = head_ref[block * BLK]
            picked_ref[block] = head
            flipped = feats.T
            pieces = []
            for s in range(sublanes):
                piece = flipped[:, s * HALF : (s + 1) * HALF].astype(jnp.float32)
                pieces.append((piece * weight[s : s + 1, :]).astype(jnp.bfloat16))
            weighted = jnp.concatenate(pieces, axis=1)
            total_ref[head] += jnp.dot(weighted, feats, preferred_element_type=jnp.float32)
            target_row = jnp.concatenate([target[s : s + 1, :] for s in range(sublanes)], axis=1)
            target_row = jnp.broadcast_to(target_row, (8, BLK)).astype(jnp.bfloat16)
            moment_ref[head] += lax.dot_general(
                target_row, weighted, (((1,), (1,)), ((), ())), preferred_element_type=jnp.float32
            )
        return carry

    lax.fori_loop(0, chunks, add_chunk, 0)
    core = core_ref[0]
    row_at, col_at = square_iotas()
    pair_ref[1, :, PART:] = jnp.zeros((2, 8, HALF), jnp.float32)
    for h in range(heads):
        second = total_ref[h, HALF:, HALF:]
        diag = jnp.sum(jnp.where(row_at == col_at, second, 0.0), axis=0, keepdims=True)
        moment = moment_ref[h, 0:1]
        extra = jnp.concatenate(
            [diag, moment[:, :HALF], moment[:, HALF:], jnp.zeros((5, HALF), jnp.float32)],
            axis=0,
        )
        merged = jnp.where(col_at <= row_at, total_ref[h, :HALF, :HALF], second)
        for q in range(2):
            pair_ref[0, q, :PART] = total_ref[h, HALF + q * PART : HALF + (q + 1) * PART, :HALF]
            pair_ref[0, q, PART:] = extra
            pair_ref[1, q, :PART] = merged[q * PART : (q + 1) * PART]
        keep_ref[2 * h : 2 * h + 2] = pair_ref[core]
        send_ref[2 * h : 2 * h + 2] = pair_ref[1 - core]


def gram_of(core, lead_heads, table, ids, targets, features):
    rows, width = features.shape
    chunks = rows // (PER_STEP * BLK)
    half = jax.ShapeDtypeStruct((2 * HEADS, PIECE, HALF), jnp.float32)
    vmem = pl.BlockSpec(memory_space=pltpu.VMEM)
    smem = pl.BlockSpec(memory_space=pltpu.SMEM)
    hbm = pl.BlockSpec(memory_space=pl.ANY)
    return pl.pallas_call(
        gram_kernel,
        out_shape=(half, half, jax.ShapeDtypeStruct((rows // BLK,), jnp.int32)),
        in_specs=[smem, hbm, vmem, vmem, vmem, hbm],
        out_specs=(vmem, vmem, smem),
        scratch_shapes=[
            pltpu.VMEM((HEADS, width, width), jnp.float32),
            pltpu.VMEM((HEADS, 8, width), jnp.float32),
            pltpu.VMEM((2, 2, PIECE, HALF), jnp.float32),
            pltpu.VMEM((rows, width), jnp.bfloat16),
            pltpu.SMEM((rows,), jnp.int32),
            pltpu.SemaphoreType.DMA((chunks,)),
            pltpu.SemaphoreType.DMA((chunks,)),
        ],
        compiler_params=pltpu.CompilerParams(vmem_limit_bytes=WIDE),
        cost_estimate=pl.CostEstimate(
            flops=2 * rows * width * width, bytes_accessed=2 * rows * width, transcendentals=0
        ),
        name="gram",
    )(core, lead_heads, table, ids, targets, features)


def plane_sum_kernel(part_ref, out_ref):
    total = part_ref[0]
    for p in range(1, part_ref.shape[0]):
        total = total + part_ref[p]
    for d in range(out_ref.shape[0]):
        out_ref[d] = total


def column_sum_kernel(part_ref, out_ref):
    total = part_ref[0:2]
    for p in range(2, part_ref.shape[0], 2):
        total = total + part_ref[p : p + 2]
    out_ref[:PART] = total[0, :PART]
    out_ref[PART:HALF] = total[1, :PART]
    out_ref[HALF:] = total[0, PART:]


def whole_call(kernel, out_shape, name, *args):
    vmem = pl.BlockSpec(memory_space=pltpu.VMEM)
    outs = jax.tree.map(lambda _: vmem, out_shape)
    return pl.pallas_call(
        kernel,
        out_shape=out_shape,
        in_specs=[vmem] * len(args),
        out_specs=outs,
        compiler_params=pltpu.CompilerParams(vmem_limit_bytes=SMALL),
        name=name,
    )(*args)


def invert_factor(sym):
    tiles = [sym[8 * t : 8 * t + 8, :] for t in range(HALF // 8)]
    lane = lax.broadcasted_iota(jnp.int32, (8, HALF), 1)
    sub = lax.broadcasted_iota(jnp.int32, (8, HALF), 0)
    rows = []
    for p in range(HALF // 8):
        inside = (lane >= 8 * p) & (lane < 8 * p + 8)
        cols = [jnp.broadcast_to(tiles[p][:, 8 * p + j : 8 * p + j + 1], (8, HALF)) for j in range(8)]
        below = {
            t: [jnp.broadcast_to(tiles[t][:, 8 * p + j : 8 * p + j + 1], (8, HALF)) for j in range(8)]
            for t in range(p + 1, HALF // 8)
        }
        panel = jnp.where(inside, jnp.where(lane == 8 * p + sub, 1.0, 0.0), tiles[p])
        for t in below:
            tiles[t] = jnp.where(inside, 0.0, tiles[t])
        pivots = jnp.ones((8, HALF), jnp.float32)
        for k in range(8):
            pivot = jnp.broadcast_to(cols[k][k : k + 1], (8, HALF))
            recip = 1.0 / pivot
            pivots = jnp.where(sub == k, pivot, pivots)
            across = [jnp.broadcast_to(cols[j][k : k + 1], (8, HALF)) for j in range(k + 1, 8)]
            row = jnp.broadcast_to(panel[k : k + 1], (8, HALF))
            if k < 7:
                scaled = jnp.where(sub > k, cols[k] * recip, 0.0)
                for j in range(k + 1, 8):
                    cols[j] = cols[j] - scaled * across[j - k - 1]
                panel = panel - scaled * row
            for t in below:
                scaled = below[t][k] * recip
                for j in range(k + 1, 8):
                    below[t][j] = below[t][j] - scaled * across[j - k - 1]
                tiles[t] = tiles[t] - scaled * row
        rows.append(jnp.where(lane <= 8 * p + sub, panel, 0.0) * lax.rsqrt(pivots))
    return jnp.concatenate(rows, axis=0)


def factor_kernel(core_ref, own_ref, other_ref, out_ref):
    row_at, col_at = square_iotas()
    eye = (row_at == col_at).astype(jnp.float32)
    first_core = core_ref[0] == 0
    own = own_ref[:HALF]
    other = other_ref[:HALF]
    cross = jnp.where(first_core, own, other)
    merged = jnp.where(first_core, other, own)
    extra = jnp.where(first_core, own_ref[HALF:], other_ref[HALF:])
    merged_t = merged.T
    first = jnp.where(col_at <= row_at, merged, merged_t) + eye
    second = jnp.where(col_at > row_at, merged, merged_t)
    second = jnp.where(col_at == row_at, extra[0:1], second) + eye
    moment1 = extra[1:2]
    moment2 = extra[2:3]
    inv1 = invert_factor(first)
    low = dot_nt(cross, inv1)
    inv2 = invert_factor(second - dot_nt(low, low))
    inv21 = -dot_nn(inv2, dot_nn(low, inv1))
    inner1 = jnp.sum(inv1 * moment1, axis=1, keepdims=True)
    inner2 = jnp.sum(inv21 * moment1 + inv2 * moment2, axis=1, keepdims=True)
    coef1 = jnp.sum(inv1 * inner1 + inv21 * inner2, axis=0, keepdims=True)
    coef2 = jnp.sum(inv2 * inner2, axis=0, keepdims=True)
    spread1 = jnp.sum(inv1 * inv1 + inv21 * inv21, axis=0, keepdims=True)
    spread2 = jnp.sum(inv2 * inv2, axis=0, keepdims=True)
    extra_out = jnp.concatenate(
        [
            jnp.sum(inv2 * eye, axis=0, keepdims=True),
            coef1 / jnp.sqrt(spread1),
            coef2 / jnp.sqrt(spread2),
            jnp.zeros((5, HALF), jnp.float32),
        ],
        axis=0,
    )
    merged_out = jnp.where(col_at <= row_at, inv1, inv2.T)
    main_out = jnp.where(first_core, inv21, merged_out)
    for p in range(out_ref.shape[0]):
        out_ref[p, :HALF] = main_out
        out_ref[p, HALF:] = extra_out


def factor_of(core, own, other):
    vmem = pl.BlockSpec(memory_space=pltpu.VMEM)
    return pl.pallas_call(
        factor_kernel,
        out_shape=jax.ShapeDtypeStruct((HEADS, PACKED, HALF), jnp.float32),
        in_specs=[pl.BlockSpec(memory_space=pltpu.SMEM), vmem, vmem],
        out_specs=vmem,
        compiler_params=pltpu.CompilerParams(vmem_limit_bytes=SMALL),
        name="factor",
    )(core, own, other)


def lever_kernel(
    lever_scale, factor_scale, picked_ref, place_ref, table_ref, id_ref, own_ref, other_ref, feats_ref,
    out_ref, score_ref, piece_ref, low_ref, full_ref, feat_ref, feat_sems,
):
    heads = low_ref.shape[0]
    piece_rows = piece_ref.shape[1]
    chunk_rows = PER_STEP * BLK
    chunks = feat_ref.shape[0] // chunk_rows
    for c in range(chunks):
        chunk_copy(c, chunk_rows, feats_ref, feat_ref, feat_sems).start()
    first_core = place_ref[1] == 0
    row_at, col_at = square_iotas()
    own_rows = pl.ds(pl.multiple_of(place_ref[0] * piece_rows, piece_rows), piece_rows)
    for h in range(heads):
        own = own_ref[h, :HALF]
        other = other_ref[h, :HALF]
        merged = jnp.where(first_core, other, own)
        second = jnp.where(col_at > row_at, merged, 0.0).T
        second = jnp.where(col_at == row_at, own_ref[h, HALF : HALF + 1], second)
        full_ref[h, :HALF, :HALF] = jnp.where(col_at <= row_at, merged, 0.0)
        full_ref[h, :HALF, HALF:] = jnp.zeros((HALF, HALF), jnp.float32)
        full_ref[h, HALF:, :HALF] = jnp.where(first_core, own, other)
        full_ref[h, HALF:, HALF:] = second
        low_ref[h] = full_ref[h].astype(jnp.bfloat16)
        score_ref[h : h + 1, :HALF] = own_ref[h, HALF + 1 : HALF + 2]
        score_ref[h : h + 1, HALF:] = own_ref[h, HALF + 2 : HALF + 3]
        piece_ref[h] = full_ref[h, own_rows, :] * factor_scale
    table = table_ref[...]
    sublanes = BLK // HALF

    def score_chunk(chunk, carry):
        chunk_copy(chunk, chunk_rows, feats_ref, feat_ref, feat_sems).wait()
        for i in range(PER_STEP):
            block = chunk * PER_STEP + i
            lines = pl.ds(pl.multiple_of(block * sublanes, sublanes), sublanes)
            weight = row_weights(table, id_ref[lines])
            projected = lax.dot_general(
                low_ref[picked_ref[block]],
                feat_ref[pl.ds(pl.multiple_of(block * BLK, BLK), BLK)],
                (((1,), (1,)), ((), ())),
                preferred_element_type=jnp.float32,
            )
            squares = jnp.sum(projected * projected, axis=0, keepdims=True)
            squares = jnp.concatenate(
                [squares[:, s * HALF : (s + 1) * HALF] for s in range(sublanes)], axis=0
            )
            out_ref[lines] = weight * squares * lever_scale
        return carry

    lax.fori_loop(0, chunks, score_chunk, 0)


def lever_of(
    picked, place, table, ids, own, other, features, lever_scale, factor_scale, piece_rows
):
    rows, width = features.shape
    vmem = pl.BlockSpec(memory_space=pltpu.VMEM)
    smem = pl.BlockSpec(memory_space=pltpu.SMEM)
    hbm = pl.BlockSpec(memory_space=pl.ANY)
    return pl.pallas_call(
        functools.partial(lever_kernel, lever_scale, factor_scale),
        out_shape=(
            jax.ShapeDtypeStruct((rows // HALF, HALF), jnp.float32),
            jax.ShapeDtypeStruct((HEADS, width), jnp.float32),
            jax.ShapeDtypeStruct((HEADS, piece_rows, width), jnp.float32),
        ),
        in_specs=[smem, smem, vmem, vmem, vmem, vmem, hbm],
        out_specs=(vmem, vmem, vmem),
        scratch_shapes=[
            pltpu.VMEM((HEADS, width, width), jnp.bfloat16),
            pltpu.VMEM((HEADS, width, width), jnp.float32),
            pltpu.VMEM((rows, width), jnp.bfloat16),
            pltpu.SemaphoreType.DMA((rows // (PER_STEP * BLK),)),
        ],
        compiler_params=pltpu.CompilerParams(vmem_limit_bytes=LARGE),
        name="lever",
    )(picked, place, table, ids, own, other, features)


def swap_cores(value):
    return lax.ppermute(value, "c", [(0, 1), (1, 0)])


def exchange(value, axes):
    return lax.all_to_all(value, axes, 0, 0, tiled=True)


def local(features, targets, station_ids, lead_heads, station_weight):
    row_count, feat_width = features.shape
    pieces = lax.axis_size(("y", "zm", "z0", "c"))
    total_rows = row_count * lax.axis_size(PLANE + COLUMN + ("c",))
    core = lax.axis_index("c").astype(jnp.int32)
    piece_at = lax.axis_index(("y", "zm", "z0", "c")).astype(jnp.int32)
    ids = station_ids.reshape(row_count // HALF, HALF)
    target_rows = targets.reshape(row_count // HALF, HALF)
    core_at = core.reshape(1)
    place = jnp.stack([piece_at, core])

    keep, send, picked = gram_of(core_at, lead_heads, station_weight, ids, target_rows, features)
    chip = keep + swap_cores(send)
    spread = whole_call(
        plane_sum_kernel,
        jax.ShapeDtypeStruct((lax.axis_size(COLUMN), PIECE, HALF), jnp.float32),
        "plane_sum",
        exchange(chip, PLANE + ("z0",)),
    )
    own = whole_call(
        column_sum_kernel,
        jax.ShapeDtypeStruct((PACKED, HALF), jnp.float32),
        "column_sum",
        exchange(spread, COLUMN),
    )
    own_inverses = exchange(factor_of(core_at, own, swap_cores(own)), PLANE)
    other_inverses = swap_cores(own_inverses)
    leverage, zscores, inverse_factor = lever_of(
        picked,
        place,
        station_weight,
        ids,
        own_inverses,
        other_inverses,
        features,
        total_rows / (HEADS * feat_width),
        math.sqrt(total_rows / HEADS),
        feat_width // pieces,
    )
    return (leverage.reshape(row_count), zscores, inverse_factor)


def solution(mesh):
    grid = Mesh(mesh.devices.reshape(4, 2, 4, 2, 2, 2), ("x", "zh", "y", "zm", "z0", "c"))
    rows = ("x", "zh", "y", "zm", "z0", "c")
    return jax.shard_map(
        local,
        mesh=grid,
        in_specs=(P(rows, None), P(rows), P(rows), P(rows), P(("x", "zh"), None)),
        out_specs=(P(rows), P(), P(None, ("y", "zm", "z0", "c"), None)),
        check_vma=False,
    )
```

```python
import functools
import math

import jax
import jax.numpy as jnp
from jax import lax
from jax.experimental import pallas as pl
from jax.experimental.pallas import tpu as pltpu
from jax.sharding import Mesh, PartitionSpec as P

HEADS = 16
BLK = 1024
PER_STEP = 4
HALF = 128
PACKED = HALF + 8
EXACT = lax.Precision.HIGHEST
PART = HALF // 2
PIECE = PART + 8
PLANE = ("x", "y")
COLUMN = ("zh", "zm", "z0")
PIECES = ("y", "zm", "z0", "c")
SMALL = 8 << 20
WIDE = 56 << 20
LARGE = 24 << 20
STAGE = 40 << 20


def dot_nn(a, b):
    return lax.dot_general(
        a, b, (((1,), (0,)), ((), ())), precision=EXACT, preferred_element_type=jnp.float32
    )


def dot_nt(a, b):
    return lax.dot_general(
        a, b, (((1,), (1,)), ((), ())), precision=EXACT, preferred_element_type=jnp.float32
    )


def square_iotas():
    row_at = lax.broadcasted_iota(jnp.int32, (HALF, HALF), 0)
    col_at = lax.broadcasted_iota(jnp.int32, (HALF, HALF), 1)
    return row_at, col_at


def row_weights(table, ids):
    return jnp.take_along_axis(jnp.broadcast_to(table, ids.shape), ids, axis=1)


def chunk_copy(chunk, rows, source_ref, target_ref, sems):
    lines = pl.ds(pl.multiple_of(chunk * rows, rows), rows)
    return pltpu.make_async_copy(source_ref.at[lines], target_ref.at[lines], sems.at[chunk])


def gram_kernel(
    lead_ref, table_ref, id_ref, target_ref, feats_ref,
    keep_ref, send_ref, picked_ref,
    total_ref, moment_ref, pair_ref, feat_ref, feat_sems,
):
    heads = total_ref.shape[0]
    chunk_rows = PER_STEP * BLK
    chunks = feat_ref.shape[0] // chunk_rows
    for c in range(chunks):
        chunk_copy(c, chunk_rows, feats_ref, feat_ref, feat_sems).start()
    total_ref[...] = jnp.zeros_like(total_ref)
    moment_ref[...] = jnp.zeros_like(moment_ref)
    table = table_ref[...]
    sublanes = BLK // HALF
    for block in range(chunks * PER_STEP):
        leads = lead_ref[block * sublanes : block * sublanes + 1].astype(jnp.float32)
        picked_ref[block] = jnp.max(leads).astype(jnp.int32)

    def add_chunk(chunk, carry):
        chunk_copy(chunk, chunk_rows, feats_ref, feat_ref, feat_sems).wait()
        for i in range(PER_STEP):
            block = chunk * PER_STEP + i
            lines = pl.ds(pl.multiple_of(block * sublanes, sublanes), sublanes)
            feats = feat_ref[pl.ds(pl.multiple_of(block * BLK, BLK), BLK)]
            weight = row_weights(table, id_ref[lines])
            target = target_ref[lines].astype(jnp.float32)
            head = picked_ref[block]
            flipped = feats.T
            pieces = []
            pulls = jnp.zeros((flipped.shape[0], HALF), jnp.float32)
            for s in range(sublanes):
                piece = flipped[:, s * HALF : (s + 1) * HALF].astype(jnp.float32)
                pieces.append((piece * weight[s : s + 1, :]).astype(jnp.bfloat16))
                pulls = pulls + pieces[-1].astype(jnp.float32) * target[s : s + 1, :]
            weighted = jnp.concatenate(pieces, axis=1)
            total_ref[head] += jnp.dot(weighted, feats, preferred_element_type=jnp.float32)
            moment_ref[head] += pulls
        return carry

    lax.fori_loop(0, chunks, add_chunk, 0)
    core = lax.axis_index("c")
    row_at, col_at = square_iotas()
    pair_ref[1, :, PART:] = jnp.zeros((2, 8, HALF), jnp.float32)
    for h in range(heads):
        second = total_ref[h, HALF:, HALF:]
        diag = jnp.sum(jnp.where(row_at == col_at, second, 0.0), axis=0, keepdims=True)
        moment = jnp.sum(moment_ref[h].T, axis=0, keepdims=True)
        extra = jnp.concatenate(
            [diag, moment[:, :HALF], moment[:, HALF:], jnp.zeros((5, HALF), jnp.float32)],
            axis=0,
        )
        merged = jnp.where(col_at <= row_at, total_ref[h, :HALF, :HALF], second)
        for q in range(2):
            pair_ref[0, q, :PART] = total_ref[h, HALF + q * PART : HALF + (q + 1) * PART, :HALF]
            pair_ref[0, q, PART:] = extra
            pair_ref[1, q, :PART] = merged[q * PART : (q + 1) * PART]
        keep_ref[2 * h : 2 * h + 2] = pair_ref[core]
        send_ref[2 * h : 2 * h + 2] = pair_ref[1 - core]


def gram_of(lead_heads, table, ids, targets, features):
    rows, width = features.shape
    chunks = rows // (PER_STEP * BLK)
    half = jax.ShapeDtypeStruct((2 * HEADS, PIECE, HALF), jnp.float32)
    vmem = pl.BlockSpec(memory_space=pltpu.VMEM)
    smem = pl.BlockSpec(memory_space=pltpu.SMEM)
    hbm = pl.BlockSpec(memory_space=pl.ANY)
    return pl.pallas_call(
        gram_kernel,
        out_shape=(half, half, jax.ShapeDtypeStruct((rows // BLK,), jnp.int32)),
        in_specs=[vmem, vmem, vmem, vmem, hbm],
        out_specs=(vmem, vmem, smem),
        scratch_shapes=[
            pltpu.VMEM((HEADS, width, width), jnp.float32),
            pltpu.VMEM((HEADS, width, HALF), jnp.float32),
            pltpu.VMEM((2, 2, PIECE, HALF), jnp.float32),
            pltpu.VMEM((rows, width), jnp.bfloat16),
            pltpu.SemaphoreType.DMA((chunks,)),
        ],
        compiler_params=pltpu.CompilerParams(vmem_limit_bytes=WIDE),
        cost_estimate=pl.CostEstimate(
            flops=2 * rows * width * width, bytes_accessed=2 * rows * width, transcendentals=0
        ),
        name="gram",
    )(lead_heads, table, ids, targets, features)


def plane_sum_kernel(part_ref, out_ref):
    total = part_ref[0]
    for p in range(1, part_ref.shape[0]):
        total = total + part_ref[p]
    for d in range(out_ref.shape[0]):
        out_ref[d] = total


def column_sum_kernel(part_ref, out_ref):
    total = part_ref[0:2]
    for p in range(2, part_ref.shape[0], 2):
        total = total + part_ref[p : p + 2]
    out_ref[:PART] = total[0, :PART]
    out_ref[PART:HALF] = total[1, :PART]
    out_ref[HALF:] = total[0, PART:]


def whole_call(kernel, out_shape, name, *args):
    vmem = pl.BlockSpec(memory_space=pltpu.VMEM)
    outs = jax.tree.map(lambda _: vmem, out_shape)
    return pl.pallas_call(
        kernel,
        out_shape=out_shape,
        in_specs=[vmem] * len(args),
        out_specs=outs,
        compiler_params=pltpu.CompilerParams(vmem_limit_bytes=SMALL),
        name=name,
    )(*args)


def invert_factor(sym):
    tiles = [sym[8 * t : 8 * t + 8, :] for t in range(HALF // 8)]
    lane = lax.broadcasted_iota(jnp.int32, (8, HALF), 1)
    sub = lax.broadcasted_iota(jnp.int32, (8, HALF), 0)
    rows = []
    for p in range(HALF // 8):
        inside = (lane >= 8 * p) & (lane < 8 * p + 8)
        cols = [jnp.broadcast_to(tiles[p][:, 8 * p + j : 8 * p + j + 1], (8, HALF)) for j in range(8)]
        below = {
            t: [jnp.broadcast_to(tiles[t][:, 8 * p + j : 8 * p + j + 1], (8, HALF)) for j in range(8)]
            for t in range(p + 1, HALF // 8)
        }
        panel = jnp.where(inside, jnp.where(lane == 8 * p + sub, 1.0, 0.0), tiles[p])
        for t in below:
            tiles[t] = jnp.where(inside, 0.0, tiles[t])
        pivots = jnp.ones((8, HALF), jnp.float32)
        for k in range(8):
            pivot = jnp.broadcast_to(cols[k][k : k + 1], (8, HALF))
            recip = 1.0 / pivot
            pivots = jnp.where(sub == k, pivot, pivots)
            across = [jnp.broadcast_to(cols[j][k : k + 1], (8, HALF)) for j in range(k + 1, 8)]
            row = jnp.broadcast_to(panel[k : k + 1], (8, HALF))
            if k < 7:
                scaled = jnp.where(sub > k, cols[k] * recip, 0.0)
                for j in range(k + 1, 8):
                    cols[j] = cols[j] - scaled * across[j - k - 1]
                panel = panel - scaled * row
            for t in below:
                scaled = below[t][k] * recip
                for j in range(k + 1, 8):
                    below[t][j] = below[t][j] - scaled * across[j - k - 1]
                tiles[t] = tiles[t] - scaled * row
        rows.append(jnp.where(lane <= 8 * p + sub, panel, 0.0) * lax.rsqrt(pivots))
    return jnp.concatenate(rows, axis=0)


def factor_kernel(own_ref, other_ref, feats_ref, out_ref, staged_ref, stage_sem):
    stage = pltpu.make_async_copy(feats_ref, staged_ref, stage_sem)
    stage.start()
    row_at, col_at = square_iotas()
    eye = (row_at == col_at).astype(jnp.float32)
    first_core = lax.axis_index("c") == 0
    own = own_ref[:HALF]
    other = other_ref[:HALF]
    cross = jnp.where(first_core, own, other)
    merged = jnp.where(first_core, other, own)
    extra = jnp.where(first_core, own_ref[HALF:], other_ref[HALF:])
    merged_t = merged.T
    first = jnp.where(col_at <= row_at, merged, merged_t) + eye
    second = jnp.where(col_at > row_at, merged, merged_t)
    second = jnp.where(col_at == row_at, extra[0:1], second) + eye
    moment1 = extra[1:2]
    moment2 = extra[2:3]
    inv1 = invert_factor(first)
    low = dot_nt(cross, inv1)
    inv2 = invert_factor(second - dot_nt(low, low))
    inv21 = -dot_nn(inv2, dot_nn(low, inv1))
    inner1 = jnp.sum(inv1 * moment1, axis=1, keepdims=True)
    inner2 = jnp.sum(inv21 * moment1 + inv2 * moment2, axis=1, keepdims=True)
    coef1 = jnp.sum(inv1 * inner1 + inv21 * inner2, axis=0, keepdims=True)
    coef2 = jnp.sum(inv2 * inner2, axis=0, keepdims=True)
    spread1 = jnp.sum(inv1 * inv1 + inv21 * inv21, axis=0, keepdims=True)
    spread2 = jnp.sum(inv2 * inv2, axis=0, keepdims=True)
    extra_out = jnp.concatenate(
        [
            jnp.sum(inv2 * eye, axis=0, keepdims=True),
            coef1 / jnp.sqrt(spread1),
            coef2 / jnp.sqrt(spread2),
            jnp.zeros((5, HALF), jnp.float32),
        ],
        axis=0,
    )
    merged_out = jnp.where(col_at <= row_at, inv1, inv2.T)
    main_out = jnp.where(first_core, inv21, merged_out)
    for p in range(out_ref.shape[0]):
        out_ref[p, :HALF] = main_out
        out_ref[p, HALF:] = extra_out
    stage.wait()


def factor_of(own, other, features):
    vmem = pl.BlockSpec(memory_space=pltpu.VMEM)
    return pl.pallas_call(
        factor_kernel,
        out_shape=(
            jax.ShapeDtypeStruct((HEADS, PACKED, HALF), jnp.float32),
            jax.ShapeDtypeStruct(features.shape, features.dtype),
        ),
        in_specs=[
            vmem,
            vmem,
            pl.BlockSpec(memory_space=pl.ANY),
        ],
        out_specs=(vmem, vmem),
        scratch_shapes=[pltpu.SemaphoreType.DMA],
        compiler_params=pltpu.CompilerParams(vmem_limit_bytes=STAGE),
        name="factor",
    )(own, other, features)


def piece_index():
    at = 0
    for axis in PIECES:
        at = at * lax.axis_size(axis) + lax.axis_index(axis)
    return at


def lever_kernel(
    lever_scale, factor_scale, picked_ref, table_ref, id_ref, own_ref, other_ref, feat_ref,
    out_ref, score_ref, piece_ref, low_ref, full_ref,
):
    heads = low_ref.shape[0]
    piece_rows = piece_ref.shape[1]
    chunks = feat_ref.shape[0] // (PER_STEP * BLK)
    first_core = lax.axis_index("c") == 0
    row_at, col_at = square_iotas()
    own_rows = pl.ds(pl.multiple_of(piece_index() * piece_rows, piece_rows), piece_rows)
    for h in range(heads):
        own = own_ref[h, :HALF]
        other = other_ref[h, :HALF]
        merged = jnp.where(first_core, other, own)
        second = jnp.where(col_at > row_at, merged, 0.0).T
        second = jnp.where(col_at == row_at, own_ref[h, HALF : HALF + 1], second)
        full_ref[h, :HALF, :HALF] = jnp.where(col_at <= row_at, merged, 0.0)
        full_ref[h, :HALF, HALF:] = jnp.zeros((HALF, HALF), jnp.float32)
        full_ref[h, HALF:, :HALF] = jnp.where(first_core, own, other)
        full_ref[h, HALF:, HALF:] = second
        low_ref[h] = full_ref[h].astype(jnp.bfloat16)
        score_ref[h : h + 1, :HALF] = own_ref[h, HALF + 1 : HALF + 2]
        score_ref[h : h + 1, HALF:] = own_ref[h, HALF + 2 : HALF + 3]
        piece_ref[h] = full_ref[h, own_rows, :] * factor_scale
    table = table_ref[...]
    sublanes = BLK // HALF

    def score_chunk(chunk, carry):
        for i in range(PER_STEP):
            block = chunk * PER_STEP + i
            lines = pl.ds(pl.multiple_of(block * sublanes, sublanes), sublanes)
            weight = row_weights(table, id_ref[lines])
            projected = lax.dot_general(
                low_ref[picked_ref[block]],
                feat_ref[pl.ds(pl.multiple_of(block * BLK, BLK), BLK)],
                (((1,), (1,)), ((), ())),
                preferred_element_type=jnp.float32,
            )
            squares = jnp.sum(projected * projected, axis=0, keepdims=True)
            squares = jnp.concatenate(
                [squares[:, s * HALF : (s + 1) * HALF] for s in range(sublanes)], axis=0
            )
            out_ref[lines] = weight * squares * lever_scale
        return carry

    lax.fori_loop(0, chunks, score_chunk, 0)


def lever_of(
    picked, table, ids, own, other, features, lever_scale, factor_scale, piece_rows
):
    rows, width = features.shape
    vmem = pl.BlockSpec(memory_space=pltpu.VMEM)
    smem = pl.BlockSpec(memory_space=pltpu.SMEM)
    return pl.pallas_call(
        functools.partial(lever_kernel, lever_scale, factor_scale),
        out_shape=(
            jax.ShapeDtypeStruct((rows // HALF, HALF), jnp.float32),
            jax.ShapeDtypeStruct((HEADS, width), jnp.float32),
            jax.ShapeDtypeStruct((HEADS, piece_rows, width), jnp.float32),
        ),
        in_specs=[smem, vmem, vmem, vmem, vmem, vmem],
        out_specs=(vmem, vmem, vmem),
        scratch_shapes=[
            pltpu.VMEM((HEADS, width, width), jnp.bfloat16),
            pltpu.VMEM((HEADS, width, width), jnp.float32),
        ],
        compiler_params=pltpu.CompilerParams(vmem_limit_bytes=LARGE),
        name="lever",
    )(picked, table, ids, own, other, features)


def swap_cores(value):
    return lax.ppermute(value, "c", [(0, 1), (1, 0)])


def exchange(value, axes):
    return lax.all_to_all(value, axes, 0, 0, tiled=True)


def local(features, targets, station_ids, lead_heads, station_weight):
    row_count, feat_width = features.shape
    pieces = lax.axis_size(PIECES)
    total_rows = row_count * lax.axis_size(PLANE + COLUMN + ("c",))
    ids = station_ids.reshape(row_count // HALF, HALF)
    lead_rows = lead_heads.reshape(row_count // HALF, HALF)
    target_rows = targets.reshape(row_count // HALF, HALF)

    keep, send, picked = gram_of(lead_rows, station_weight, ids, target_rows, features)
    chip = keep + swap_cores(send)
    partial = whole_call(
        plane_sum_kernel,
        jax.ShapeDtypeStruct((lax.axis_size(COLUMN), PIECE, HALF), jnp.float32),
        "plane_sum",
        exchange(chip, PLANE + ("z0",)),
    )
    own = whole_call(
        column_sum_kernel,
        jax.ShapeDtypeStruct((PACKED, HALF), jnp.float32),
        "column_sum",
        exchange(partial, COLUMN),
    )
    spread, staged = factor_of(own, swap_cores(own), features)
    own_inverses = exchange(spread, PLANE)
    other_inverses = swap_cores(own_inverses)
    leverage, zscores, inverse_factor = lever_of(
        picked,
        station_weight,
        ids,
        own_inverses,
        other_inverses,
        staged,
        total_rows / (HEADS * feat_width),
        math.sqrt(total_rows / HEADS),
        feat_width // pieces,
    )
    return (leverage.reshape(row_count), zscores, inverse_factor)


def solution(mesh):
    grid = Mesh(mesh.devices.reshape(4, 2, 4, 2, 2, 2), ("x", "zh", "y", "zm", "z0", "c"))
    rows = ("x", "zh", "y", "zm", "z0", "c")
    return jax.shard_map(
        local,
        mesh=grid,
        in_specs=(P(rows, None), P(rows), P(rows), P(rows), P(("x", "zh"), None)),
        out_specs=(P(rows), P(), P(None, PIECES, None)),
        check_vma=False,
    )
```

```python
import functools
import math

import jax
import jax.numpy as jnp
from jax import lax
from jax.experimental import pallas as pl
from jax.experimental.pallas import tpu as pltpu
from jax.sharding import Mesh, PartitionSpec as P

HEADS = 16
BLK = 1024
PER_STEP = 4
HALF = 128
PACKED = HALF + 8
EXACT = lax.Precision.HIGHEST
PART = HALF // 2
PIECE = PART + 8
PLANE = ("x", "y")
COLUMN = ("zh", "zm", "z0")
PIECES = ("y", "zm", "z0", "c")
SMALL = 8 << 20
WIDE = 61 << 20
LARGE = 24 << 20


def dot_nn(a, b):
    return lax.dot_general(
        a, b, (((1,), (0,)), ((), ())), precision=EXACT, preferred_element_type=jnp.float32
    )


def dot_nt(a, b):
    return lax.dot_general(
        a, b, (((1,), (1,)), ((), ())), precision=EXACT, preferred_element_type=jnp.float32
    )


def square_iotas():
    row_at = lax.broadcasted_iota(jnp.int32, (HALF, HALF), 0)
    col_at = lax.broadcasted_iota(jnp.int32, (HALF, HALF), 1)
    return row_at, col_at


def row_weights(table, ids):
    return jnp.take_along_axis(jnp.broadcast_to(table, ids.shape), ids, axis=1)


def chunk_copy(chunk, rows, source_ref, target_ref, sems):
    lines = pl.ds(pl.multiple_of(chunk * rows, rows), rows)
    return pltpu.make_async_copy(source_ref.at[lines], target_ref.at[lines], sems.at[chunk])


def gram_kernel(
    lead_ref, table_ref, id_ref, target_ref, feats_ref,
    keep_ref, send_ref, picked_ref,
    total_ref, moment_ref, pair_ref, feat_ref, feat_sems,
):
    heads = total_ref.shape[0]
    chunk_rows = PER_STEP * BLK
    chunks = feat_ref.shape[0] // chunk_rows
    for c in range(chunks):
        chunk_copy(c, chunk_rows, feats_ref, feat_ref, feat_sems).start()
    total_ref[...] = jnp.zeros_like(total_ref)
    moment_ref[...] = jnp.zeros_like(moment_ref)
    table = table_ref[...]
    sublanes = BLK // HALF
    for block in range(chunks * PER_STEP):
        leads = lead_ref[block * sublanes : block * sublanes + 1].astype(jnp.float32)
        picked_ref[block] = jnp.max(leads).astype(jnp.int32)

    def add_chunk(chunk, carry):
        chunk_copy(chunk, chunk_rows, feats_ref, feat_ref, feat_sems).wait()
        for i in range(PER_STEP):
            block = chunk * PER_STEP + i
            lines = pl.ds(pl.multiple_of(block * sublanes, sublanes), sublanes)
            feats = feat_ref[pl.ds(pl.multiple_of(block * BLK, BLK), BLK)]
            weight = row_weights(table, id_ref[lines])
            target = target_ref[lines].astype(jnp.float32)
            head = picked_ref[block]
            flipped = feats.T
            pieces = []
            pulls = jnp.zeros((flipped.shape[0], HALF), jnp.float32)
            for s in range(sublanes):
                piece = flipped[:, s * HALF : (s + 1) * HALF].astype(jnp.float32)
                pieces.append((piece * weight[s : s + 1, :]).astype(jnp.bfloat16))
                pulls = pulls + pieces[-1].astype(jnp.float32) * target[s : s + 1, :]
            weighted = jnp.concatenate(pieces, axis=1)
            total_ref[head] += jnp.dot(weighted, feats, preferred_element_type=jnp.float32)
            moment_ref[head] += pulls
        return carry

    lax.fori_loop(0, chunks, add_chunk, 0)
    core = lax.axis_index("c")
    row_at, col_at = square_iotas()
    pair_ref[1, :, PART:] = jnp.zeros((2, 8, HALF), jnp.float32)
    for h in range(heads):
        second = total_ref[h, HALF:, HALF:]
        diag = jnp.sum(jnp.where(row_at == col_at, second, 0.0), axis=0, keepdims=True)
        moment = jnp.sum(moment_ref[h].T, axis=0, keepdims=True)
        extra = jnp.concatenate(
            [diag, moment[:, :HALF], moment[:, HALF:], jnp.zeros((5, HALF), jnp.float32)],
            axis=0,
        )
        merged = jnp.where(col_at <= row_at, total_ref[h, :HALF, :HALF], second)
        for q in range(2):
            pair_ref[0, q, :PART] = total_ref[h, HALF + q * PART : HALF + (q + 1) * PART, :HALF]
            pair_ref[0, q, PART:] = extra
            pair_ref[1, q, :PART] = merged[q * PART : (q + 1) * PART]
        keep_ref[2 * h : 2 * h + 2] = pair_ref[core]
        send_ref[2 * h : 2 * h + 2] = pair_ref[1 - core]


def gram_of(lead_heads, table, ids, targets, features):
    rows, width = features.shape
    chunks = rows // (PER_STEP * BLK)
    half = jax.ShapeDtypeStruct((2 * HEADS, PIECE, HALF), jnp.float32)
    vmem = pl.BlockSpec(memory_space=pltpu.VMEM)
    smem = pl.BlockSpec(memory_space=pltpu.SMEM)
    hbm = pl.BlockSpec(memory_space=pl.ANY)
    return pl.pallas_call(
        gram_kernel,
        out_shape=(half, half, jax.ShapeDtypeStruct((rows // BLK,), jnp.int32)),
        in_specs=[vmem, vmem, vmem, vmem, hbm],
        out_specs=(vmem, vmem, smem),
        scratch_shapes=[
            pltpu.VMEM((HEADS, width, width), jnp.float32),
            pltpu.VMEM((HEADS, width, HALF), jnp.float32),
            pltpu.VMEM((2, 2, PIECE, HALF), jnp.float32),
            pltpu.VMEM((rows, width), jnp.bfloat16),
            pltpu.SemaphoreType.DMA((chunks,)),
        ],
        compiler_params=pltpu.CompilerParams(vmem_limit_bytes=WIDE),
        cost_estimate=pl.CostEstimate(
            flops=2 * rows * width * width, bytes_accessed=2 * rows * width, transcendentals=0
        ),
        name="gram",
    )(lead_heads, table, ids, targets, features)


def plane_sum_kernel(part_ref, out_ref):
    total = part_ref[0]
    for p in range(1, part_ref.shape[0]):
        total = total + part_ref[p]
    for d in range(out_ref.shape[0]):
        out_ref[d] = total


def column_sum_kernel(part_ref, out_ref):
    total = part_ref[0:2]
    for p in range(2, part_ref.shape[0], 2):
        total = total + part_ref[p : p + 2]
    out_ref[:PART] = total[0, :PART]
    out_ref[PART:HALF] = total[1, :PART]
    out_ref[HALF:] = total[0, PART:]


def whole_call(kernel, out_shape, name, *args):
    vmem = pl.BlockSpec(memory_space=pltpu.VMEM)
    outs = jax.tree.map(lambda _: vmem, out_shape)
    return pl.pallas_call(
        kernel,
        out_shape=out_shape,
        in_specs=[vmem] * len(args),
        out_specs=outs,
        compiler_params=pltpu.CompilerParams(vmem_limit_bytes=SMALL),
        name=name,
    )(*args)


def invert_factor(sym):
    tiles = [sym[8 * t : 8 * t + 8, :] for t in range(HALF // 8)]
    lane = lax.broadcasted_iota(jnp.int32, (8, HALF), 1)
    sub = lax.broadcasted_iota(jnp.int32, (8, HALF), 0)
    rows = []
    for p in range(HALF // 8):
        inside = (lane >= 8 * p) & (lane < 8 * p + 8)
        cols = [jnp.broadcast_to(tiles[p][:, 8 * p + j : 8 * p + j + 1], (8, HALF)) for j in range(8)]
        below = {
            t: [jnp.broadcast_to(tiles[t][:, 8 * p + j : 8 * p + j + 1], (8, HALF)) for j in range(8)]
            for t in range(p + 1, HALF // 8)
        }
        panel = jnp.where(inside, jnp.where(lane == 8 * p + sub, 1.0, 0.0), tiles[p])
        for t in below:
            tiles[t] = jnp.where(inside, 0.0, tiles[t])
        pivots = jnp.ones((8, HALF), jnp.float32)
        for k in range(8):
            pivot = jnp.broadcast_to(cols[k][k : k + 1], (8, HALF))
            recip = 1.0 / pivot
            pivots = jnp.where(sub == k, pivot, pivots)
            across = [jnp.broadcast_to(cols[j][k : k + 1], (8, HALF)) for j in range(k + 1, 8)]
            row = jnp.broadcast_to(panel[k : k + 1], (8, HALF))
            if k < 7:
                scaled = jnp.where(sub > k, cols[k] * recip, 0.0)
                for j in range(k + 1, 8):
                    cols[j] = cols[j] - scaled * across[j - k - 1]
                panel = panel - scaled * row
            for t in below:
                scaled = below[t][k] * recip
                for j in range(k + 1, 8):
                    below[t][j] = below[t][j] - scaled * across[j - k - 1]
                tiles[t] = tiles[t] - scaled * row
        rows.append(jnp.where(lane <= 8 * p + sub, panel, 0.0) * lax.rsqrt(pivots))
    return jnp.concatenate(rows, axis=0)


def factor_kernel(own_ref, other_ref, out_ref):
    row_at, col_at = square_iotas()
    eye = (row_at == col_at).astype(jnp.float32)
    first_core = lax.axis_index("c") == 0
    own = own_ref[:HALF]
    other = other_ref[:HALF]
    cross = jnp.where(first_core, own, other)
    merged = jnp.where(first_core, other, own)
    extra = jnp.where(first_core, own_ref[HALF:], other_ref[HALF:])
    merged_t = merged.T
    first = jnp.where(col_at <= row_at, merged, merged_t) + eye
    second = jnp.where(col_at > row_at, merged, merged_t)
    second = jnp.where(col_at == row_at, extra[0:1], second) + eye
    moment1 = extra[1:2]
    moment2 = extra[2:3]
    inv1 = invert_factor(first)
    low = dot_nt(cross, inv1)
    inv2 = invert_factor(second - dot_nt(low, low))
    inv21 = -dot_nn(inv2, dot_nn(low, inv1))
    inner1 = jnp.sum(inv1 * moment1, axis=1, keepdims=True)
    inner2 = jnp.sum(inv21 * moment1 + inv2 * moment2, axis=1, keepdims=True)
    coef1 = jnp.sum(inv1 * inner1 + inv21 * inner2, axis=0, keepdims=True)
    coef2 = jnp.sum(inv2 * inner2, axis=0, keepdims=True)
    spread1 = jnp.sum(inv1 * inv1 + inv21 * inv21, axis=0, keepdims=True)
    spread2 = jnp.sum(inv2 * inv2, axis=0, keepdims=True)
    extra_out = jnp.concatenate(
        [
            jnp.sum(inv2 * eye, axis=0, keepdims=True),
            coef1 / jnp.sqrt(spread1),
            coef2 / jnp.sqrt(spread2),
            jnp.zeros((5, HALF), jnp.float32),
        ],
        axis=0,
    )
    merged_out = jnp.where(col_at <= row_at, inv1, inv2.T)
    main_out = jnp.where(first_core, inv21, merged_out)
    for p in range(out_ref.shape[0]):
        out_ref[p, :HALF] = main_out
        out_ref[p, HALF:] = extra_out


def factor_of(own, other):
    vmem = pl.BlockSpec(memory_space=pltpu.VMEM)
    return pl.pallas_call(
        factor_kernel,
        out_shape=jax.ShapeDtypeStruct((HEADS, PACKED, HALF), jnp.float32),
        in_specs=[vmem, vmem],
        out_specs=vmem,
        compiler_params=pltpu.CompilerParams(vmem_limit_bytes=SMALL),
        name="factor",
    )(own, other)


def piece_index():
    at = 0
    for axis in PIECES:
        at = at * lax.axis_size(axis) + lax.axis_index(axis)
    return at


def lever_kernel(
    lever_scale, factor_scale, picked_ref, table_ref, id_ref, own_ref, other_ref, feat_ref,
    out_ref, score_ref, piece_ref, low_ref, full_ref,
):
    heads = low_ref.shape[0]
    piece_rows = piece_ref.shape[1]
    chunks = feat_ref.shape[0] // (PER_STEP * BLK)
    first_core = lax.axis_index("c") == 0
    row_at, col_at = square_iotas()
    own_rows = pl.ds(pl.multiple_of(piece_index() * piece_rows, piece_rows), piece_rows)
    for h in range(heads):
        own = own_ref[h, :HALF]
        other = other_ref[h, :HALF]
        merged = jnp.where(first_core, other, own)
        second = jnp.where(col_at > row_at, merged, 0.0).T
        second = jnp.where(col_at == row_at, own_ref[h, HALF : HALF + 1], second)
        full_ref[h, :HALF, :HALF] = jnp.where(col_at <= row_at, merged, 0.0)
        full_ref[h, :HALF, HALF:] = jnp.zeros((HALF, HALF), jnp.float32)
        full_ref[h, HALF:, :HALF] = jnp.where(first_core, own, other)
        full_ref[h, HALF:, HALF:] = second
        low_ref[h] = full_ref[h].astype(jnp.bfloat16)
        score_ref[h : h + 1, :HALF] = own_ref[h, HALF + 1 : HALF + 2]
        score_ref[h : h + 1, HALF:] = own_ref[h, HALF + 2 : HALF + 3]
        piece_ref[h] = full_ref[h, own_rows, :] * factor_scale
    table = table_ref[...]
    sublanes = BLK // HALF

    def score_chunk(chunk, carry):
        for i in range(PER_STEP):
            block = chunk * PER_STEP + i
            lines = pl.ds(pl.multiple_of(block * sublanes, sublanes), sublanes)
            weight = row_weights(table, id_ref[lines])
            projected = lax.dot_general(
                low_ref[picked_ref[block]],
                feat_ref[pl.ds(pl.multiple_of(block * BLK, BLK), BLK)],
                (((1,), (1,)), ((), ())),
                preferred_element_type=jnp.float32,
            )
            squares = jnp.sum(projected * projected, axis=0, keepdims=True)
            squares = jnp.concatenate(
                [squares[:, s * HALF : (s + 1) * HALF] for s in range(sublanes)], axis=0
            )
            out_ref[lines] = weight * squares * lever_scale
        return carry

    lax.fori_loop(0, chunks, score_chunk, 0)


def lever_of(
    picked, table, ids, own, other, features, lever_scale, factor_scale, piece_rows
):
    rows, width = features.shape
    vmem = pl.BlockSpec(memory_space=pltpu.VMEM)
    smem = pl.BlockSpec(memory_space=pltpu.SMEM)
    return pl.pallas_call(
        functools.partial(lever_kernel, lever_scale, factor_scale),
        out_shape=(
            jax.ShapeDtypeStruct((rows // HALF, HALF), jnp.float32),
            jax.ShapeDtypeStruct((HEADS, width), jnp.float32),
            jax.ShapeDtypeStruct((HEADS, piece_rows, width), jnp.float32),
        ),
        in_specs=[smem, vmem, vmem, vmem, vmem, vmem],
        out_specs=(vmem, vmem, vmem),
        scratch_shapes=[
            pltpu.VMEM((HEADS, width, width), jnp.bfloat16),
            pltpu.VMEM((HEADS, width, width), jnp.float32),
        ],
        compiler_params=pltpu.CompilerParams(vmem_limit_bytes=LARGE),
        name="lever",
    )(picked, table, ids, own, other, features)


def swap_cores(value):
    return lax.ppermute(value, "c", [(0, 1), (1, 0)])


def exchange(value, axes):
    return lax.all_to_all(value, axes, 0, 0, tiled=True)


def local(features, targets, station_ids, lead_heads, station_weight):
    row_count, feat_width = features.shape
    pieces = lax.axis_size(PIECES)
    total_rows = row_count * lax.axis_size(PLANE + COLUMN + ("c",))
    ids = station_ids.reshape(row_count // HALF, HALF)
    lead_rows = lead_heads.reshape(row_count // HALF, HALF)
    target_rows = targets.reshape(row_count // HALF, HALF)

    keep, send, picked = gram_of(lead_rows, station_weight, ids, target_rows, features)
    chip = keep + swap_cores(send)
    partial = whole_call(
        plane_sum_kernel,
        jax.ShapeDtypeStruct((lax.axis_size(COLUMN), PIECE, HALF), jnp.float32),
        "plane_sum",
        exchange(chip, PLANE + ("z0",)),
    )
    own = whole_call(
        column_sum_kernel,
        jax.ShapeDtypeStruct((PACKED, HALF), jnp.float32),
        "column_sum",
        exchange(partial, COLUMN),
    )
    own_inverses = exchange(factor_of(own, swap_cores(own)), PLANE)
    other_inverses = swap_cores(own_inverses)
    leverage, zscores, inverse_factor = lever_of(
        picked,
        station_weight,
        ids,
        own_inverses,
        other_inverses,
        features,
        total_rows / (HEADS * feat_width),
        math.sqrt(total_rows / HEADS),
        feat_width // pieces,
    )
    return (leverage.reshape(row_count), zscores, inverse_factor)


def solution(mesh):
    grid = Mesh(mesh.devices.reshape(4, 2, 4, 2, 2, 2), ("x", "zh", "y", "zm", "z0", "c"))
    rows = ("x", "zh", "y", "zm", "z0", "c")
    return jax.shard_map(
        local,
        mesh=grid,
        in_specs=(P(rows, None), P(rows), P(rows), P(rows), P(("x", "zh"), None)),
        out_specs=(P(rows), P(), P(None, PIECES, None)),
        check_vma=False,
    )
```
